256 devices in a mesh: tm: 32 (over y, x, core), rows: 8 (over z).
Axes of the slice: x: 4, y: 4, z: 8, core: 2. Of those that a mesh axis runs over, the one named last changes fastest.
Arguments:
- tokens: bfloat16 [32, 64, 64, 768], P('tm', 'rows'), may hold values from -6 to 6
- col_shift: int32 [32], P('tm'), may hold values from 0 to 7
- frame_group: int32 [32], replicated, may hold values from 0 to 15, never falling along the last dimension, each value on 1 to 4 neighbouring positions
- spatial_qkv: bfloat16 [768, 2304], replicated
- spatial_out: bfloat16 [768, 768], replicated
- temporal_qkv: bfloat16 [768, 2304], replicated
- temporal_out: bfloat16 [768, 768], replicated, may hold values from -0.21875 to 0.21875
Outputs:
- layer_out: bfloat16 [32, 64, 64, 768], P('tm', 'rows')
The draws below stay inside these ranges and needn't reach their ends.
Inputs may be any that keep to these rules, and one draw needn't show every extreme that they name: `frame_group`: never falls from one frame to the next and every group from 0 on appears.
All inputs are finite; a program needn't handle non-finite values.
Results may differ from the reference program's by a relative error of at most 0.008.
The reference program's roundings to bfloat16 on the way count: a program that leaves them out, or rounds other values in their place, can miss the bound.
Values may be sent and summed in bfloat16 or wider, within the bound.
A program may use at most 64 MiB of HBM per device.

```python
import math
import jax
import jax.numpy as jnp
import numpy as np
from jax import lax

D = 768
HEADS = 12
HD = 64
WIN = 8
COLS = 64
FRAMES = 32
ROWS_ALL = 64


def draw_tokens(key, part):
    full_shape = (FRAMES, ROWS_ALL, COLS, D)
    values = jax.random.normal(jax.random.fold_in(key, 3), full_shape, jnp.float32)
    return jnp.clip(values, -6.0, 6.0).astype(jnp.bfloat16)


def projection_draw(key, salt):
    values = jax.random.normal(jax.random.fold_in(key, salt), (D, 3 * D), jnp.float32) / math.sqrt(D)
    return values.astype(jnp.bfloat16)


def draw_spatial_qkv(key, part):
    return projection_draw(key, 5)


def draw_temporal_qkv(key, part):
    return projection_draw(key, 13)


def draw_spatial_out(key, part):
    values = jax.random.normal(jax.random.fold_in(key, 7), (D, D), jnp.float32) / math.sqrt(D)
    return values.astype(jnp.bfloat16)


def touch_ends(entries, stream_key, smallest, largest):
    place = [jax.random.randint(jax.random.fold_in(stream_key, axis), (), 0, length) for axis, length in enumerate(entries.shape)]
    main_axis = entries.shape.index(max(entries.shape))
    next_to = place[:main_axis] + [(place[main_axis] + 1) % entries.shape[main_axis]] + place[main_axis + 1:]
    return entries.at[tuple(place)].set(smallest).at[tuple(next_to)].set(largest)


def split_up(amount, total, bound, slope):
    portions = [(1 << 20) // math.isqrt(standing ** slope) + 1 for standing in range(2, amount + 1)]
    rest, given = total - bound - (amount - 1), [1] * (amount - 1)
    while rest > 0:
        free = [i for i in range(amount - 1) if given[i] < bound]
        whole, remaining = sum([portions[i] for i in free]), rest
        for i in free:
            extra = min(bound - given[i], max(1, remaining * portions[i] // whole), rest)
            given[i] = given[i] + extra
            rest = rest - extra
    return np.array([bound] + given)


def uneven(stream_key, amount, total, most, lean):
    if amount == 2:
        one = jax.random.randint(stream_key, (), max(1, total - most), min(most, total - 1) + 1)
        return jnp.stack([one, total - one])
    lengths = jnp.asarray(split_up(amount, total, most, lean), jnp.int32)
    twos = (amount - 1) // 2
    giver, receiver = lengths[1:1 + 2 * twos:2], lengths[2:2 + 2 * twos:2]
    margin = jnp.minimum(giver - 1, most - receiver)
    passed = jax.random.randint(jax.random.fold_in(stream_key, 1), (twos,), 0, 1 << 20) % (margin + 1)
    lengths = lengths.at[1:1 + 2 * twos:2].set(giver - passed).at[2:2 + 2 * twos:2].set(receiver + passed)
    return lengths[jax.random.permutation(jax.random.fold_in(stream_key, 2), amount)]


def noise(key, extent, scale, reach, kind=jnp.bfloat16):
    drawn = scale * jax.random.normal(key, extent, jnp.float32)
    return jnp.clip(drawn, min=-reach, max=reach).astype(kind)


def setup_inputs(seed: int = 0) -> dict:
    key_of = jax.random.split(jax.random.key(seed), 8)
    tokens = draw_tokens(jax.random.fold_in(key_of[7], 71), 0)
    col_shift = touch_ends(jax.random.randint(key_of[1], (FRAMES,), 0, WIN), jax.random.fold_in(key_of[1], 1), 0, WIN - 1).astype(jnp.int32)
    frame_group = jnp.searchsorted(jnp.cumsum(uneven(key_of[2], FRAMES // 2, FRAMES, 4, 0)), jnp.arange(FRAMES), side="right").astype(jnp.int32)
    spatial_qkv = draw_spatial_qkv(jax.random.fold_in(key_of[7], 71), 0)
    spatial_out = draw_spatial_out(jax.random.fold_in(key_of[7], 71), 0)
    temporal_qkv = draw_temporal_qkv(jax.random.fold_in(key_of[7], 71), 0)
    temporal_out = noise(key_of[6], (D, D), D ** -0.5, 0.21875)
    return {"tokens": tokens, "col_shift": col_shift, "frame_group": frame_group, "spatial_qkv": spatial_qkv, "spatial_out": spatial_out, "temporal_qkv": temporal_qkv, "temporal_out": temporal_out}


def normalize(values):
    widened = values.astype(jnp.float32)
    center = widened - lax.optimization_barrier(jnp.mean(widened, axis=-1, keepdims=True))
    spread = lax.optimization_barrier(jnp.mean(center * center, axis=-1, keepdims=True))
    return (center * lax.rsqrt(spread + 1e-05)).astype(jnp.bfloat16)

def project(values, weight):
    flattened = values.reshape(-1, values.shape[-1])
    product = jnp.dot(flattened, weight, preferred_element_type=jnp.float32)
    return product.reshape(values.shape[:-1] + (weight.shape[1],))

def attend(queries, key_rows, value_rows, allowed):
    scale = 1.0 / math.sqrt(queries.shape[-1])
    scores = jnp.einsum('bnhd,bmhd->bhnm', queries.astype(jnp.float32), key_rows.astype(jnp.float32)) * scale
    if allowed is not None:
        scores = jnp.where(allowed, scores, -1e+30)
    maxima = lax.optimization_barrier(jnp.max(scores, axis=-1, keepdims=True))
    raised = jnp.exp(scores - maxima)
    totals = lax.optimization_barrier(jnp.sum(raised, axis=-1, keepdims=True))
    weights = (raised / totals).astype(jnp.bfloat16)
    mixed_rows = jnp.einsum('bhnm,bmhd->bnhd', weights.astype(jnp.float32), value_rows.astype(jnp.float32))
    return mixed_rows.astype(jnp.bfloat16)

def spatial_frame(single_frame, offset, weight_in, weight_out):
    height = single_frame.shape[0]
    columns = single_frame.shape[1]
    half_window = WIN // 2
    projected = project(normalize(single_frame), weight_in).astype(jnp.bfloat16)
    rolled = jnp.roll(jnp.roll(projected, -half_window, axis=0), -offset, axis=1)
    windowed = rolled.reshape(height // WIN, WIN, columns // WIN, WIN, 3, HEADS, HD)
    windowed = windowed.transpose(0, 2, 1, 3, 4, 5, 6).reshape(-1, WIN * WIN, 3, HEADS, HD)
    attended = attend(windowed[:, :, 0], windowed[:, :, 1], windowed[:, :, 2], None)
    attended = attended.reshape(height // WIN, columns // WIN, WIN, WIN, D)
    attended = attended.transpose(0, 2, 1, 3, 4).reshape(height, columns, D)
    restored = jnp.roll(jnp.roll(attended, offset, axis=1), half_window, axis=0)
    branch = project(restored, weight_out)
    return (single_frame.astype(jnp.float32) + branch).astype(jnp.bfloat16)

def reference(tokens, col_shift, frame_group, spatial_qkv, spatial_out, temporal_qkv, temporal_out):

    def frame_step(frame_inputs):
        return spatial_frame(frame_inputs[0], frame_inputs[1], spatial_qkv, spatial_out)
    stream = lax.map(frame_step, (tokens, col_shift))
    allowed = frame_group[None, :] <= frame_group[:, None]

    def temporal_row(rows_in):
        frames_all = rows_in.shape[0]
        columns = rows_in.shape[1]
        projected = project(normalize(rows_in), temporal_qkv).astype(jnp.bfloat16)
        projected = projected.reshape(frames_all, columns, 3, HEADS, HD).transpose(1, 0, 2, 3, 4)
        attended = attend(projected[:, :, 0], projected[:, :, 1], projected[:, :, 2], allowed)
        attended = attended.transpose(1, 0, 2, 3).reshape(frames_all, columns, D)
        return (rows_in.astype(jnp.float32) + project(attended, temporal_out)).astype(jnp.bfloat16)
    layer_rows = lax.map(temporal_row, stream.transpose(1, 0, 2, 3))
    return layer_rows.transpose(1, 0, 2, 3)
```

```python
import jax
import jax.numpy as jnp
from jax import lax
from jax.experimental import pallas as pl
from jax.experimental.pallas import tpu as pltpu
from jax.sharding import PartitionSpec as P

D = 768
GROUP = 256
BF16 = jnp.bfloat16
F32 = jnp.float32
MESH = pl.DeviceIdType.MESH


def iota(shape, dim):
    return lax.broadcasted_iota(jnp.int32, shape, dim)


def one_hot(mask):
    return jnp.where(mask, 1.0, 0.0).astype(BF16)


def layer_norm(x):
    center = x - jnp.mean(x, axis=-1, keepdims=True)
    spread = jnp.mean(center * center, axis=-1, keepdims=True)
    return (center * lax.rsqrt(spread + 1e-05)).astype(BF16)


def dot(a, b):
    return jnp.dot(a, b, preferred_element_type=F32)


def dot_t(a, b):
    return lax.dot_general(a, b, (((1,), (1,)), ((), ())), preferred_element_type=F32)


def block_diagonal(x):
    lane = iota(x.shape, 1) // 64
    return jnp.concatenate([jnp.where(lane == h, x, jnp.zeros_like(x)) for h in range(4)], axis=0)


def spread_heads(reduce, s, fill):
    parts = []
    for half in range(2):
        part = s[:, half * 128 : half * 128 + 128]
        low = iota(part.shape, 1) < 64
        first = reduce(jnp.where(low, part, fill), axis=-1, keepdims=True)
        second = reduce(jnp.where(low, fill, part), axis=-1, keepdims=True)
        parts.append(jnp.where(low, first, second))
    return jnp.concatenate(parts, axis=1)


def attend(q, k, v, allowed):
    s = dot_t(q, block_diagonal(k))
    if allowed is not None:
        s = jnp.where(allowed, s, -1e30)
    top = spread_heads(jnp.max, s, -jnp.inf)
    e = jnp.exp((s - top) * 0.125)
    total = spread_heads(jnp.sum, e, 0.0)
    weights = (e / total).astype(BF16)
    return dot(weights, block_diagonal(v)).astype(BF16)


def kernel(
    shift_ref, group_ref, tok, wsq_h, wso_h, wtq_h, wto_h, out,
    wsq, wso, wtq, wto, town, trcv, xin, qown, qrcv, mix, sbuf, rbuf, qt, mixt, xout, obuf, mask,
    lsem, osem, zs, zr, fs, fr, bs, br,
):
    tm = lax.axis_index("tm")
    z = lax.axis_index("rows")
    core = lax.rem(tm, 2)
    x = lax.rem(tm // 2, 4)
    y = tm // 8
    column = lax.rem(tm, 8)
    zup = lax.rem(z + 1 + 6 * core, 8)
    zdown = lax.rem(z + 7 + 2 * core, 8)

    def block(i):
        return lax.rem(2 * x + 1 + i, 8)

    loads = [
        pltpu.make_async_copy(src, dst, lsem.at[n])
        for n, (src, dst) in enumerate(((wsq_h, wsq), (wso_h, wso), (wtq_h, wtq), (wto_h, wto)))
    ]

    def own_copy(i):
        return pltpu.make_async_copy(
            tok.at[pl.ds(4 - 4 * core, 4), block(i)], town.at[i], osem.at[i]
        )

    @pl.loop(0, 8)
    def _(i):
        own_copy(i).start()

    for load in loads:
        load.start()

    barrier = pltpu.get_barrier_semaphore()

    @pl.loop(1, 32)
    def _(n):
        pl.semaphore_signal(
            barrier, inc=1, device_id=(lax.rem(tm + n, 32), z), device_id_type=MESH
        )

    sender_core = y // 2
    sender_z = lax.rem(z + 7 + 2 * sender_core, 8)

    @pl.loop(0, 16)
    def _(n):
        pl.semaphore_signal(
            barrier, inc=1, device_id=(2 * n + sender_core, sender_z), device_id_type=MESH
        )

    pl.semaphore_signal(barrier, inc=1, device_id=(tm, zup), device_id_type=MESH)

    shift = shift_ref[0]

    rows, cols = iota((64, 96), 0), iota((64, 96), 1)
    gather = one_hot(
        (lax.rem(rows // 8, 4) == lax.rem(cols // 8, 4))
        & (8 * (cols // 32) + lax.rem(cols, 8) == 8 * (rows // 32) + lax.rem(rows, 8) + shift)
    )
    rows, cols = iota((128, 192), 0), iota((128, 192), 1)
    scatter = one_hot(
        (lax.rem(rows // 8, 8) == lax.rem(cols // 8, 8))
        & (8 * (rows // 64) + lax.rem(rows, 8) + 8 == 8 * (cols // 64) + lax.rem(cols, 8) + shift)
    )

    def normed_pair(buffer, t):
        parts = []
        for b in range(3):
            parts.append(buffer[lax.rem(2 * t + b, 8)].astype(F32).reshape(32, D))
        normed = layer_norm(jnp.concatenate(parts, axis=0))
        return dot(gather, normed).astype(BF16)

    @pl.loop(0, 8)
    def _(i):
        own_copy(i).wait()

    @pl.loop(0, 4)
    def _(t):
        xin[pl.ds(pl.multiple_of(t * 64, 64), 64), :] = normed_pair(town, t)

    loads[0].wait()

    def project_own(n):
        lanes = pl.ds(pl.multiple_of(n * GROUP, GROUP), GROUP)
        qown[:, lanes] = dot(xin[...], wsq[:, lanes]).astype(BF16)

    pl.loop(0, 9)(project_own)

    mix[0:64, :] = jnp.zeros((64, D), BF16)

    q_row, k_col = iota((64, 1), 0), lax.rem(iota((1, GROUP), 1), 64)

    def frame_of(n):
        m = lax.rem(n, 8)
        return (m // 2) * 8 + (n // 16) * 2 + lax.rem(m, 2)

    q_frame, k_frame = frame_of(q_row), frame_of(k_col)
    q_group, k_group = jnp.zeros_like(q_frame), jnp.zeros_like(k_frame)
    for f in range(32):
        value = group_ref[f]
        q_group = jnp.where(q_frame == f, value, q_group)
        k_group = jnp.where(k_frame == f, value, k_group)
    same = lax.rem(q_row // 8, 2) == lax.rem(k_col // 8, 2)
    mask[...] = jnp.where(same & (k_group <= q_group), 1, 0)

    pl.semaphore_wait(barrier, 48)

    def z_copy(i):
        return pltpu.make_async_remote_copy(
            src_ref=tok.at[pl.ds(4 * core, 4), block(i)],
            dst_ref=trcv.at[i],
            send_sem=zs.at[i],
            recv_sem=zr.at[i],
            device_id=(tm, zdown),
            device_id_type=MESH,
        )

    @pl.loop(0, 8)
    def _(i):
        z_copy(i).start()

    for load in loads[1:]:
        load.wait()

    def forward(i, h, u, act):
        half = core if h else 1 - core
        target = (2 * half + u) * 8 + block(i)
        target_z = zup if h else z
        source = sbuf.at[i, h, pl.ds(2 * u, 2)]
        place = rbuf.at[x, 2 * y + core]
        number = i * 4 + h * 2 + u
        remote = pltpu.make_async_remote_copy(
            src_ref=source,
            dst_ref=place,
            send_sem=fs.at[number],
            recv_sem=fr.at[x],
            device_id=(target, target_z),
            device_id_type=MESH,
        )
        if h:
            act(remote, None)
        else:
            here = target == tm

            @pl.when(here)
            def _():
                act(None, pltpu.make_async_copy(source, place, fr.at[x]))

            @pl.when(jnp.logical_not(here))
            def _():
                act(remote, None)

    def start(remote, local):
        (remote if local is None else local).start()

    def finish(remote, local):
        if local is None:
            remote.wait_send()

    def send_block(i):
        for h in range(2):
            for u in range(2):
                forward(i, h, u, start)

    def finish_blocks(first, count, mixed, matrix):
        flat = dot(matrix, mixed).astype(BF16)
        y_out = dot(flat, wso[...])
        residual = []
        for n in range(count):
            for buffer in (town, trcv):
                residual.append(buffer[first + n].astype(F32).reshape(32, D))
        stream = (jnp.concatenate(residual, axis=0) + y_out).astype(BF16)
        for n in range(count):
            for h in range(2):
                at = (2 * n + h) * 32
                for r in range(4):
                    sbuf[first + n, h, r] = stream[at + 8 * r : at + 8 * r + 8, :]

    z_copy(0).wait_recv()

    @pl.loop(0, 4)
    def _(t):
        z_copy(2 * t + 1).wait_recv()

        @pl.when(t < 3)
        def _():
            z_copy(2 * t + 2).wait_recv()

        received = normed_pair(trcv, t)
        for n in range(9):
            lanes = slice(n * GROUP, n * GROUP + GROUP)
            qrcv[:, lanes] = dot(received, wsq[:, lanes]).astype(BF16)
        for w in range(2):
            own_rows = pl.ds(pl.multiple_of(t * 64 + w * 32, 32), 32)
            for g in range(3):

                def part(n):
                    lanes = slice(n * D + g * GROUP, n * D + g * GROUP + GROUP)
                    return jnp.concatenate(
                        [qown[own_rows, lanes], qrcv[w * 32 : w * 32 + 32, lanes]], axis=0
                    )

                mixed = attend(part(0), part(1), part(2), None)
                at = pl.ds(pl.multiple_of((2 * t + w + 1) * 64, 64), 64)
                mix[at, g * GROUP : g * GROUP + GROUP] = mixed
        recent = mix[pl.ds(pl.multiple_of(t * 128, 128), 192), :]
        finish_blocks(2 * t, 2, recent, scatter)

        @pl.when(t > 0)
        def _():
            send_block(2 * t)

        send_block(2 * t + 1)

    edge = jnp.concatenate([mix[512:576, :], mix[64:128, :]], axis=0)
    finish_blocks(0, 1, edge, scatter[:64, :128])
    send_block(0)

    rows, cols = iota((128, 128), 0), iota((128, 128), 1)
    regroup = one_hot((rows // 8 == lax.rem(cols, 16)) & (lax.rem(rows, 8) == cols // 16))
    rows, cols = iota((64, 64), 0), iota((64, 64), 1)
    swap = one_hot((rows // 8 == lax.rem(cols, 8)) & (lax.rem(rows, 8) == cols // 8))

    @pl.loop(0, 4)
    def _(n):
        source = lax.rem(x + 3 - n, 4)
        pltpu.make_async_copy(rbuf.at[source], rbuf.at[source], fr.at[source]).wait()
        normed = layer_norm(rbuf[source].astype(F32).reshape(128, D))
        ordered = dot(regroup, normed).astype(BF16)
        for m in range(9):
            lanes = slice(m * GROUP, m * GROUP + GROUP)
            qt[source, :, lanes] = dot(ordered, wtq[:, lanes]).astype(BF16)

    def give_back(r, source, m, act):
        target = (m // 2) * 8 + source * 2 + lax.rem(m, 2)
        data = obuf.at[r, source, m]
        place = out.at[2 * y + r, column]
        here = target == tm

        @pl.when(here)
        def _():
            act(None, pltpu.make_async_copy(data, place, br))

        @pl.when(jnp.logical_not(here))
        def _():
            act(
                pltpu.make_async_remote_copy(
                    src_ref=data,
                    dst_ref=place,
                    send_sem=bs.at[r * 32 + source * 8 + m],
                    recv_sem=br,
                    device_id=(target, z),
                    device_id_type=MESH,
                ),
                None,
            )

    @pl.loop(0, 2)
    def _(r):
        @pl.loop(0, 2)
        def _(pair):
            for lp in range(2):
                at = pl.ds(pl.multiple_of(r * 64 + pair * 32 + lp * 16, 16), 16)
                for g in range(3):

                    def part(n):
                        lanes = slice(n * D + g * GROUP, n * D + g * GROUP + GROUP)
                        return jnp.concatenate([qt[s, at, lanes] for s in range(4)], axis=0)

                    mixed = attend(part(0), part(1), part(2), mask[...] != 0)
                    for s in range(4):
                        mixt[s, at, g * GROUP : g * GROUP + GROUP] = mixed[s * 16 : s * 16 + 16, :]

        for s in range(4):
            half = mixt[s, pl.ds(pl.multiple_of(r * 64, 64), 64), :]
            xout[s * 64 : s * 64 + 64, :] = dot(swap, half).astype(BF16)
        for n in range(3):
            lanes = slice(n * GROUP, n * GROUP + GROUP)
            branch = dot(xout[...], wto[:, lanes])
            residual = rbuf[:, :, r, :, lanes].astype(F32).reshape(256, GROUP)
            obuf[r, :, :, :, lanes] = (residual + branch).reshape(4, 8, 8, GROUP).astype(BF16)

        @pl.loop(0, 4)
        def _(n):
            source = lax.rem(x + 1 + n, 4)

            @pl.loop(0, 8)
            def _(m):
                give_back(r, source, m, start)

    pltpu.make_async_copy(out, out, br).wait()

    @pl.loop(0, 8)
    def _(i):
        z_copy(i).wait_send()
        for h in range(2):
            for u in range(2):
                forward(i, h, u, finish)

    @pl.loop(0, 2)
    def _(r):
        @pl.loop(0, 4)
        def _(s):
            @pl.loop(0, 8)
            def _(m):
                give_back(r, s, m, finish)


def per_device(
    tokens, col_shift, frame_group, spatial_qkv, spatial_out, temporal_qkv, temporal_out
):
    smem = pl.BlockSpec(memory_space=pltpu.SMEM)
    anywhere = pl.BlockSpec(memory_space=pl.ANY)
    dma = pltpu.SemaphoreType.DMA
    result = pl.pallas_call(
        kernel,
        out_shape=jax.ShapeDtypeStruct((8, 8, 8, D), BF16),
        in_specs=[smem, smem] + [anywhere] * 5,
        out_specs=anywhere,
        scratch_shapes=[
            pltpu.VMEM((D, 3 * D), BF16),
            pltpu.VMEM((D, D), BF16),
            pltpu.VMEM((D, 3 * D), BF16),
            pltpu.VMEM((D, D), BF16),
            pltpu.VMEM((8, 4, 8, D), BF16),
            pltpu.VMEM((8, 4, 8, D), BF16),
            pltpu.VMEM((256, D), BF16),
            pltpu.VMEM((256, 3 * D), BF16),
            pltpu.VMEM((64, 3 * D), BF16),
            pltpu.VMEM((576, D), BF16),
            pltpu.VMEM((8, 2, 4, 8, D), BF16),
            pltpu.VMEM((4, 8, 2, 8, D), BF16),
            pltpu.VMEM((4, 128, 3 * D), BF16),
            pltpu.VMEM((4, 128, D), BF16),
            pltpu.VMEM((256, D), BF16),
            pltpu.VMEM((2, 4, 8, 8, D), BF16),
            pltpu.VMEM((64, GROUP), jnp.int32),
            dma((4,)),
            dma((8,)),
            dma((8,)),
            dma((8,)),
            dma((32,)),
            dma((4,)),
            dma((64,)),
            dma,
        ],
        compiler_params=pltpu.CompilerParams(
            collective_id=0, has_side_effects=True, vmem_limit_bytes=56 * 1024 * 1024
        ),
    )(
        col_shift,
        frame_group,
        tokens.reshape(8, 8, 8, D),
        spatial_qkv,
        spatial_out,
        temporal_qkv,
        temporal_out,
    )
    return result.reshape(tokens.shape)


def solution(mesh):
    in_specs = (P("tm", "rows", None, None), P("tm"), P(), P(), P(), P(), P())
    out_specs = P("tm", "rows", None, None)
    return jax.shard_map(
        per_device, mesh=mesh, in_specs=in_specs, out_specs=out_specs, check_vma=False
    )
```

```python
import jax
import jax.numpy as jnp
from jax import lax
from jax.experimental import pallas as pl
from jax.experimental.pallas import tpu as pltpu
from jax.sharding import PartitionSpec as P

D = 768
GROUP = 256
BF16 = jnp.bfloat16
F32 = jnp.float32
MESH = pl.DeviceIdType.MESH
AHEAD = 2
BEHIND = 2


def iota(shape, dim):
    return lax.broadcasted_iota(jnp.int32, shape, dim)


def one_hot(mask):
    return jnp.where(mask, 1.0, 0.0).astype(BF16)


def layer_norm(x):
    center = x - jnp.mean(x, axis=-1, keepdims=True)
    spread = jnp.mean(center * center, axis=-1, keepdims=True)
    return (center * lax.rsqrt(spread + 1e-05)).astype(BF16)


def dot(a, b):
    return jnp.dot(a, b, preferred_element_type=F32)


def dot_t(a, b):
    return lax.dot_general(a, b, (((1,), (1,)), ((), ())), preferred_element_type=F32)


def block_diagonal(x):
    lane = iota(x.shape, 1) // 64
    return jnp.concatenate([jnp.where(lane == h, x, jnp.zeros_like(x)) for h in range(4)], axis=0)


def attend(s):
    e = jnp.exp((s - jnp.max(s, axis=0, keepdims=True)) * 0.125)
    return (e * (1.0 / jnp.sum(e, axis=0, keepdims=True))).astype(BF16)


def attend_all(bodies, allowed, same_head):
    def scores(body):
        s = dot_t(body[1](), block_diagonal(body[0]()))
        return s if allowed is None else jnp.where(allowed, s, -1e30)

    waiting, ready = [scores(body) for body in bodies[:AHEAD]], []
    for n, body in enumerate(bodies):
        if n + AHEAD < len(bodies):
            waiting.append(scores(bodies[n + AHEAD]))
        ready.append(attend(waiting[n]))
        if n >= BEHIND:
            mix_values(ready[n - BEHIND], *bodies[n - BEHIND][2:], same_head)
    for n in range(len(bodies) - BEHIND, len(bodies)):
        mix_values(ready[n], *bodies[n][2:], same_head)


def mix_values(weights, values, slot, store, same_head):
    values = values()
    blank = jnp.zeros_like(weights)
    padded = jnp.concatenate([blank, weights] if slot else [weights, blank], axis=0)
    for p in range(2):
        lanes = slice(p * 128, p * 128 + 128)
        mixed = dot(values[lanes, :], padded[:, lanes])
        store(p, jnp.where(same_head, mixed, 0.0).astype(BF16))


def kernel(
    shift_ref, group_ref, tok, wsq_h, wso_h, wtq_h, wto_h, out,
    wsq, wso, wtq, wto, wsv, wtv, town, trcv, xin, qown, qrcv, values, mix, sbuf, rbuf, normed_t, qt,
    mixt, xout, obuf, mask, lsem, osem, zs, zr, fs, fr, bs, br,
):
    tm = lax.axis_index("tm")
    z = lax.axis_index("rows")
    core = lax.rem(tm, 2)
    x = lax.rem(tm // 2, 4)
    y = tm // 8
    column = lax.rem(tm, 8)
    zup = lax.rem(z + 1 + 6 * core, 8)
    zdown = lax.rem(z + 7 + 2 * core, 8)

    def block(i):
        return lax.rem(2 * x + 1 + i, 8)

    loads = [
        pltpu.make_async_copy(src, dst, lsem.at[n])
        for n, (src, dst) in enumerate(((wsq_h, wsq), (wso_h, wso), (wtq_h, wtq), (wto_h, wto)))
    ]

    def own_copy(i):
        return pltpu.make_async_copy(
            tok.at[pl.ds(4 - 4 * core, 4), block(i)], town.at[i], osem.at[i]
        )

    @pl.loop(0, 8)
    def _(i):
        own_copy(i).start()

    for load in loads:
        load.start()

    barrier = pltpu.get_barrier_semaphore()

    @pl.loop(1, 32)
    def _(n):
        pl.semaphore_signal(
            barrier, inc=1, device_id=(lax.rem(tm + n, 32), z), device_id_type=MESH
        )

    sender_core = y // 2
    sender_z = lax.rem(z + 7 + 2 * sender_core, 8)

    @pl.loop(0, 16)
    def _(n):
        pl.semaphore_signal(
            barrier, inc=1, device_id=(2 * n + sender_core, sender_z), device_id_type=MESH
        )

    pl.semaphore_signal(barrier, inc=1, device_id=(tm, zup), device_id_type=MESH)

    shift = shift_ref[0]

    rows, cols = iota((64, 96), 0), iota((64, 96), 1)
    gather = one_hot(
        (lax.rem(rows // 8, 4) == lax.rem(cols // 8, 4))
        & (8 * (cols // 32) + lax.rem(cols, 8) == 8 * (rows // 32) + lax.rem(rows, 8) + shift)
    )
    rows, cols = iota((128, 384), 0), iota((128, 384), 1)
    scatter = one_hot(
        (lax.rem(rows // 8, 8) == lax.rem(cols // 8, 8))
        & (8 * (rows // 64) + lax.rem(rows, 8) + 8 == 8 * (cols // 128) + lax.rem(cols, 8) + shift)
    )
    same_head = iota((128, 128), 0) // 64 == iota((128, 128), 1) // 64
    unit = one_hot(iota((GROUP, GROUP), 0) == iota((GROUP, GROUP), 1))

    def transpose_values(weight, result):
        @pl.loop(0, 3)
        def _(i):
            rows_out = pl.ds(pl.multiple_of(i * GROUP, GROUP), GROUP)
            lanes = pl.ds(pl.multiple_of(2 * D + i * GROUP, GROUP), GROUP)
            for j in range(3):
                part = slice(j * GROUP, j * GROUP + GROUP)
                result[rows_out, part] = dot_t(unit, weight[part, lanes]).astype(BF16)

    def normed_pair(buffer, t):
        parts = []
        for b in range(3):
            parts.append(buffer[lax.rem(2 * t + b, 8)].astype(F32).reshape(32, D))
        normed = layer_norm(jnp.concatenate(parts, axis=0))
        return dot(gather, normed).astype(BF16)

    @pl.loop(0, 8)
    def _(i):
        own_copy(i).wait()

    @pl.loop(0, 4)
    def _(t):
        xin[pl.ds(pl.multiple_of(t * 64, 64), 64), :] = normed_pair(town, t)

    loads[0].wait()

    def project_own(n):
        lanes = pl.ds(pl.multiple_of(n * GROUP, GROUP), GROUP)
        qown[:, lanes] = dot(xin[...], wsq[:, lanes]).astype(BF16)

    pl.loop(0, 6)(project_own)
    transpose_values(wsq, wsv)

    for p in range(6):
        mix[p, :, 0:128] = jnp.zeros((128, 128), BF16)

    k_row, q_col = iota((64, 1), 0), lax.rem(iota((1, GROUP), 1), 64)

    def frame_of(n):
        m = lax.rem(n, 8)
        return (m // 2) * 8 + (n // 16) * 2 + lax.rem(m, 2)

    k_frame, q_frame = frame_of(k_row), frame_of(q_col)
    q_group, k_group = jnp.zeros_like(q_frame), jnp.zeros_like(k_frame)
    for f in range(32):
        value = group_ref[f]
        q_group = jnp.where(q_frame == f, value, q_group)
        k_group = jnp.where(k_frame == f, value, k_group)
    same = lax.rem(k_row // 8, 2) == lax.rem(q_col // 8, 2)
    mask[...] = jnp.where(same & (k_group <= q_group), 1, 0)

    pl.semaphore_wait(barrier, 48)

    def z_copy(i):
        return pltpu.make_async_remote_copy(
            src_ref=tok.at[pl.ds(4 * core, 4), block(i)],
            dst_ref=trcv.at[i],
            send_sem=zs,
            recv_sem=zr.at[i],
            device_id=(tm, zdown),
            device_id_type=MESH,
        )

    @pl.loop(0, 8)
    def _(i):
        z_copy(i).start()

    for load in loads[1:]:
        load.wait()
    transpose_values(wtq, wtv)

    def send_block(i):
        for h in range(2):
            for u in range(2):
                half = core if h else 1 - core
                target = (2 * half + u) * 8 + block(i)
                source = sbuf.at[i * 4 + h * 2 + u]
                place = rbuf.at[x, 2 * y + core]
                remote = pltpu.make_async_remote_copy(
                    src_ref=source,
                    dst_ref=place,
                    send_sem=fs,
                    recv_sem=fr.at[x],
                    device_id=(target, zup if h else z),
                    device_id_type=MESH,
                )
                if h:
                    remote.start()
                else:
                    here = target == tm

                    @pl.when(here)
                    def _():
                        pltpu.make_async_copy(source, place, fr.at[x]).start()

                    pl.when(jnp.logical_not(here))(remote.start)

    def finish_blocks(first, count, mixed, matrix):
        flat = jnp.concatenate([dot_t(matrix, part).astype(BF16) for part in mixed], axis=1)
        y_out = dot(flat, wso[...])
        residual = []
        for n in range(count):
            for buffer in (town, trcv):
                residual.append(buffer[first + n].astype(F32).reshape(32, D))
        stream = (jnp.concatenate(residual, axis=0) + y_out).astype(BF16)
        for n in range(count):
            for h in range(2):
                at = (2 * n + h) * 32
                for r in range(4):
                    chunk = (first + n) * 4 + h * 2 + r // 2
                    sbuf[chunk, r % 2] = stream[at + 8 * r : at + 8 * r + 8, :]

    z_copy(0).wait_recv()

    @pl.loop(0, 4)
    def _(t):
        z_copy(2 * t + 1).wait_recv()

        @pl.when(t < 3)
        def _():
            z_copy(2 * t + 2).wait_recv()

        received = normed_pair(trcv, t)
        own_pair = xin[pl.ds(pl.multiple_of(t * 64, 64), 64), :]
        pair = jnp.concatenate(
            [own_pair[:32], received[:32], own_pair[32:], received[32:]], axis=0
        )
        for n in range(3):
            part_rows = slice(n * GROUP, n * GROUP + GROUP)
            values[part_rows, :] = dot_t(wsv[part_rows, :], pair).astype(BF16)
        for n in range(6):
            lanes = slice(n * GROUP, n * GROUP + GROUP)
            qrcv[:, lanes] = dot(received, wsq[:, lanes]).astype(BF16)
        def window(w, g):
            own_rows = pl.ds(pl.multiple_of(t * 64 + w * 32, 32), 32)

            def part(n):
                lanes = slice(n * D + g * GROUP, n * D + g * GROUP + GROUP)
                return jnp.concatenate(
                    [qown[own_rows, lanes], qrcv[w * 32 : w * 32 + 32, lanes]], axis=0
                )

            def store(p, mixed):
                at = pl.ds(pl.multiple_of((2 * t + w + 1) * 128, 128), 128)
                mix[2 * g + p, :, at] = mixed

            def group_values():
                return values[g * GROUP : g * GROUP + GROUP, :]

            return lambda: part(0), lambda: part(1), group_values, w, store

        attend_all([window(w, g) for w in range(2) for g in range(3)], None, same_head)
        last_three = pl.ds(pl.multiple_of(t * 256, 256), 384)
        recent = [mix[p, :, last_three] for p in range(6)]
        finish_blocks(2 * t, 2, recent, scatter)

        @pl.when(t > 0)
        def _():
            send_block(2 * t)

        send_block(2 * t + 1)

    edge = [jnp.concatenate([mix[p, :, 1024:1152], mix[p, :, 128:256]], axis=1) for p in range(6)]
    finish_blocks(0, 1, edge, scatter[:64, :256])
    send_block(0)

    rows, cols = iota((128, 128), 0), iota((128, 128), 1)
    regroup = one_hot((rows // 8 == lax.rem(cols, 16)) & (lax.rem(rows, 8) == cols // 16))
    rows, cols = iota((256, 512), 0), iota((256, 512), 1)
    swap = one_hot(
        (rows // 64 == lax.rem(cols // 16, 4))
        & (lax.rem(rows // 8, 8) == lax.rem(cols, 8))
        & (lax.rem(rows, 8) == 2 * (cols // 128) + lax.rem(cols // 8, 2))
    )

    @pl.loop(0, 4)
    def _(n):
        source = lax.rem(x + 3 - n, 4)
        pltpu.make_async_copy(rbuf.at[source], rbuf.at[source], fr.at[source]).wait()
        normed = layer_norm(rbuf[source].astype(F32).reshape(128, D))
        ordered = dot(regroup, normed).astype(BF16)
        normed_t[source] = ordered
        for m in range(6):
            lanes = slice(m * GROUP, m * GROUP + GROUP)
            qt[source, :, lanes] = dot(ordered, wtq[:, lanes]).astype(BF16)

    @pl.loop(0, 2)
    def _(r):
        @pl.loop(0, 2)
        def _(pair):
            def at(lp):
                return pl.ds(pl.multiple_of(r * 64 + pair * 32 + lp * 16, 16), 16)

            tokens_pair = jnp.concatenate(
                [normed_t[s, at(lp), :] for lp in range(2) for s in range(4)], axis=0
            )
            for n in range(3):
                part_rows = slice(n * GROUP, n * GROUP + GROUP)
                values[part_rows, :] = dot_t(wtv[part_rows, :], tokens_pair).astype(BF16)
            def location(lp, g):
                def part(n):
                    lanes = slice(n * D + g * GROUP, n * D + g * GROUP + GROUP)
                    return jnp.concatenate([qt[s, at(lp), lanes] for s in range(4)], axis=0)

                def store(p, mixed):
                    place = pl.ds(pl.multiple_of((2 * pair + lp) * 128, 128), 128)
                    mixt[2 * g + p, :, place] = mixed

                def group_values():
                    return values[g * GROUP : g * GROUP + GROUP, :]

                return lambda: part(0), lambda: part(1), group_values, lp, store

            bodies = [location(lp, g) for lp in range(2) for g in range(3)]
            attend_all(bodies, mask[...] != 0, same_head)

        for p in range(6):
            xout[:, p * 128 : p * 128 + 128] = dot_t(swap, mixt[p]).astype(BF16)
        for n in range(3):
            lanes = slice(n * GROUP, n * GROUP + GROUP)
            branch = dot(xout[...], wto[:, lanes])
            residual = rbuf[:, :, r, :, lanes].astype(F32).reshape(256, GROUP)
            result = (residual + branch).astype(BF16)
            for k in range(32):
                frame = (k % 8) // 2 * 8 + k // 8 * 2 + k % 2
                obuf[r * 32 + frame, :, lanes] = result[k * 8 : k * 8 + 8, :]

        place = out.at[2 * y + r, column]

        @pl.loop(1, 32)
        def _(n):
            target = lax.rem(tm + n, 32)
            pltpu.make_async_remote_copy(
                src_ref=obuf.at[r * 32 + target],
                dst_ref=place,
                send_sem=bs,
                recv_sem=br,
                device_id=(target, z),
                device_id_type=MESH,
            ).start()

        pltpu.make_async_copy(obuf.at[r * 32 + tm], place, br).start()

    def wait_bytes(ref, sem):
        pltpu.make_async_copy(ref, ref, sem).wait()

    wait_bytes(out, br)
    wait_bytes(trcv, zs)
    local = y // 2 == 1 - core

    @pl.when(local)
    def _():
        wait_bytes(sbuf.at[pl.ds(0, 31)], fs)

    @pl.when(jnp.logical_not(local))
    def _():
        wait_bytes(sbuf, fs)

    wait_bytes(obuf.at[pl.ds(0, 62)], bs)


def per_device(
    tokens, col_shift, frame_group, spatial_qkv, spatial_out, temporal_qkv, temporal_out
):
    smem = pl.BlockSpec(memory_space=pltpu.SMEM)
    anywhere = pl.BlockSpec(memory_space=pl.ANY)
    dma = pltpu.SemaphoreType.DMA
    result = pl.pallas_call(
        kernel,
        out_shape=jax.ShapeDtypeStruct((8, 8, 8, D), BF16),
        in_specs=[smem, smem] + [anywhere] * 5,
        out_specs=anywhere,
        scratch_shapes=[
            pltpu.VMEM((D, 3 * D), BF16),
            pltpu.VMEM((D, D), BF16),
            pltpu.VMEM((D, 3 * D), BF16),
            pltpu.VMEM((D, D), BF16),
            pltpu.VMEM((D, D), BF16),
            pltpu.VMEM((D, D), BF16),
            pltpu.VMEM((8, 4, 8, D), BF16),
            pltpu.VMEM((8, 4, 8, D), BF16),
            pltpu.VMEM((256, D), BF16),
            pltpu.VMEM((256, 2 * D), BF16),
            pltpu.VMEM((64, 2 * D), BF16),
            pltpu.VMEM((D, 128), BF16),
            pltpu.VMEM((6, 128, 9 * 128), BF16),
            pltpu.VMEM((32, 2, 8, D), BF16),
            pltpu.VMEM((4, 8, 2, 8, D), BF16),
            pltpu.VMEM((4, 128, D), BF16),
            pltpu.VMEM((4, 128, 2 * D), BF16),
            pltpu.VMEM((6, 128, 512), BF16),
            pltpu.VMEM((256, D), BF16),
            pltpu.VMEM((64, 8, D), BF16),
            pltpu.VMEM((64, GROUP), jnp.int32),
            dma((4,)),
            dma((8,)),
            dma,
            dma((8,)),
            dma,
            dma((4,)),
            dma,
            dma,
        ],
        compiler_params=pltpu.CompilerParams(
            collective_id=0, has_side_effects=True, vmem_limit_bytes=56 * 1024 * 1024
        ),
    )(
        col_shift,
        frame_group,
        tokens.reshape(8, 8, 8, D),
        spatial_qkv,
        spatial_out,
        temporal_qkv,
        temporal_out,
    )
    return result.reshape(tokens.shape)


def solution(mesh):
    in_specs = (P("tm", "rows", None, None), P("tm"), P(), P(), P(), P(), P())
    out_specs = P("tm", "rows", None, None)
    return jax.shard_map(
        per_device, mesh=mesh, in_specs=in_specs, out_specs=out_specs, check_vma=False
    )
```

```python
import functools

import jax
import jax.numpy as jnp
from jax import lax
from jax.experimental import pallas as pl
from jax.experimental.pallas import tpu as pltpu
from jax.sharding import PartitionSpec as P

D = 768
GROUP = 256
BF16 = jnp.bfloat16
F32 = jnp.float32
MESH = pl.DeviceIdType.MESH
AHEAD = 2
BEHIND = 2


def iota(shape, dim):
    return lax.broadcasted_iota(jnp.int32, shape, dim)


def one_hot(mask):
    return jnp.where(mask, 1.0, 0.0).astype(BF16)


def layer_norm(x):
    center = x - jnp.mean(x, axis=-1, keepdims=True)
    spread = jnp.mean(center * center, axis=-1, keepdims=True)
    return (center * lax.rsqrt(spread + 1e-05)).astype(BF16)


def dot(a, b):
    return jnp.dot(a, b, preferred_element_type=F32)


def dot_t(a, b):
    return lax.dot_general(a, b, (((1,), (1,)), ((), ())), preferred_element_type=F32)


def block_diagonal(x):
    lane = iota(x.shape, 1) // 64
    return jnp.concatenate([jnp.where(lane == h, x, jnp.zeros_like(x)) for h in range(4)], axis=0)


def attend(s):
    e = jnp.exp((s - jnp.max(s, axis=0, keepdims=True)) * 0.125)
    return (e * (1.0 / jnp.sum(e, axis=0, keepdims=True))).astype(BF16)


def attend_all(bodies, allowed, same_head, extra=()):
    extra = list(extra)
    share = -(-len(extra) // len(bodies))
    def scores(body):
        s = dot_t(body[1](), block_diagonal(body[0]()))
        return s if allowed is None else jnp.where(allowed, s, -1e30)

    waiting, ready = [scores(body) for body in bodies[:AHEAD]], []
    for n, body in enumerate(bodies):
        if n + AHEAD < len(bodies):
            waiting.append(scores(bodies[n + AHEAD]))
        ready.append(attend(waiting[n]))
        if n >= BEHIND:
            mix_values(ready[n - BEHIND], *bodies[n - BEHIND][2:], same_head)
        for work in extra[n * share : n * share + share]:
            work()
    for n in range(len(bodies) - BEHIND, len(bodies)):
        mix_values(ready[n], *bodies[n][2:], same_head)


def mix_values(weights, values, slot, store, same_head):
    values = values()
    blank = jnp.zeros_like(weights)
    padded = jnp.concatenate([blank, weights] if slot else [weights, blank], axis=0)
    for p in range(2):
        lanes = slice(p * 128, p * 128 + 128)
        mixed = dot(values[lanes, :], padded[:, lanes])
        store(p, jnp.where(same_head, mixed, 0.0).astype(BF16))


def kernel(
    shift_ref, group_ref, tok, wsq_h, wso_h, wtq_h, wto_h, out,
    wsq, wso, wtq, wto, wsv, wtv, town, trcv, xin, qown, qrcv, values, mix, sbuf, rbuf, normed_t, qt,
    mixt, xout, obuf, mask, lsem, osem, zs, zr, fs, fr, bs, br,
):
    tm = lax.axis_index("tm")
    z = lax.axis_index("rows")
    core = lax.rem(tm, 2)
    x = lax.rem(tm // 2, 4)
    y = tm // 8
    column = lax.rem(tm, 8)
    zup = lax.rem(z + 1 + 6 * core, 8)
    zdown = lax.rem(z + 7 + 2 * core, 8)

    def block(i):
        return lax.rem(2 * x + 1 + i, 8)

    loads = [
        pltpu.make_async_copy(src, dst, lsem.at[n])
        for n, (src, dst) in enumerate(((wsq_h, wsq), (wso_h, wso), (wtq_h, wtq), (wto_h, wto)))
    ]

    def own_copy(i):
        return pltpu.make_async_copy(
            tok.at[pl.ds(4 - 4 * core, 4), block(i)], town.at[i], osem.at[i]
        )

    @pl.loop(0, 8)
    def _(i):
        own_copy(i).start()

    loads[0].start()
    loads[1].start()

    barrier = pltpu.get_barrier_semaphore()
    pl.semaphore_signal(barrier, inc=1, device_id=(tm, zup), device_id_type=MESH)

    @pl.loop(1, 32)
    def _(n):
        pl.semaphore_signal(
            barrier, inc=1, device_id=(lax.rem(tm + n, 32), z), device_id_type=MESH
        )

    sender_core = y // 2
    sender_z = lax.rem(z + 7 + 2 * sender_core, 8)

    @pl.loop(0, 16)
    def _(n):
        pl.semaphore_signal(
            barrier, inc=1, device_id=(2 * n + sender_core, sender_z), device_id_type=MESH
        )

    shift = shift_ref[0]

    rows, cols = iota((64, 96), 0), iota((64, 96), 1)
    gather = one_hot(
        (lax.rem(rows // 8, 4) == lax.rem(cols // 8, 4))
        & (8 * (cols // 32) + lax.rem(cols, 8) == 8 * (rows // 32) + lax.rem(rows, 8) + shift)
    )
    rows, cols = iota((128, 384), 0), iota((128, 384), 1)
    scatter = one_hot(
        (lax.rem(rows // 8, 8) == lax.rem(cols // 8, 8))
        & (8 * (rows // 64) + lax.rem(rows, 8) + 8 == 8 * (cols // 128) + lax.rem(cols, 8) + shift)
    )
    same_head = iota((128, 128), 0) // 64 == iota((128, 128), 1) // 64
    unit = one_hot(iota((GROUP, GROUP), 0) == iota((GROUP, GROUP), 1))

    def transpose_values(weight, result):
        @pl.loop(0, 3)
        def _(i):
            rows_out = pl.ds(pl.multiple_of(i * GROUP, GROUP), GROUP)
            lanes = pl.ds(pl.multiple_of(2 * D + i * GROUP, GROUP), GROUP)
            for j in range(3):
                part = slice(j * GROUP, j * GROUP + GROUP)
                result[rows_out, part] = dot_t(unit, weight[part, lanes]).astype(BF16)

    def normed_pair(buffer, t):
        parts = []
        for b in range(3):
            parts.append(buffer[(2 * t + b) % 8 if isinstance(t, int) else lax.rem(2 * t + b, 8)].astype(F32).reshape(32, D))
        normed = layer_norm(jnp.concatenate(parts, axis=0))
        return dot(gather, normed).astype(BF16)

    @pl.loop(0, 8)
    def _(i):
        own_copy(i).wait()

    @pl.loop(0, 4)
    def _(t):
        xin[pl.ds(pl.multiple_of(t * 64, 64), 64), :] = normed_pair(town, t)

    pl.semaphore_wait(barrier, 48)

    def z_copy(i):
        return pltpu.make_async_remote_copy(
            src_ref=tok.at[pl.ds(4 * core, 4), block(i)],
            dst_ref=trcv.at[i],
            send_sem=zs,
            recv_sem=zr.at[i],
            device_id=(tm, zdown),
            device_id_type=MESH,
        )

    @pl.loop(0, 8)
    def _(i):
        z_copy(i).start()

    loads[0].wait()
    loads[2].start()
    loads[3].start()

    def project_own(n):
        lanes = pl.ds(pl.multiple_of(n * GROUP, GROUP), GROUP)
        qown[:, lanes] = dot(xin[...], wsq[:, lanes]).astype(BF16)

    pl.loop(0, 6)(project_own)
    transpose_values(wsq, wsv)

    for p in range(6):
        mix[p, :, 0:128] = jnp.zeros((128, 128), BF16)

    k_row, q_col = iota((64, 1), 0), lax.rem(iota((1, GROUP), 1), 64)

    def frame_of(n):
        m = lax.rem(n, 8)
        return (m // 2) * 8 + (n // 16) * 2 + lax.rem(m, 2)

    k_frame, q_frame = frame_of(k_row), frame_of(q_col)
    q_group, k_group = jnp.zeros_like(q_frame), jnp.zeros_like(k_frame)
    for f in range(32):
        value = group_ref[f]
        q_group = jnp.where(q_frame == f, value, q_group)
        k_group = jnp.where(k_frame == f, value, k_group)
    same = lax.rem(k_row // 8, 2) == lax.rem(q_col // 8, 2)
    mask[...] = jnp.where(same & (k_group <= q_group), 1, 0)

    loads[1].wait()

    def send_block(i):
        for h in range(2):
            for u in range(2):
                half = core if h else 1 - core
                target = (2 * half + u) * 8 + block(i)
                source = sbuf.at[i * 4 + h * 2 + u]
                place = rbuf.at[x, 2 * y + core]
                remote = pltpu.make_async_remote_copy(
                    src_ref=source,
                    dst_ref=place,
                    send_sem=fs,
                    recv_sem=fr.at[x],
                    device_id=(target, zup if h else z),
                    device_id_type=MESH,
                )
                if h or 0 < i < 7:
                    remote.start()
                else:
                    here = target == tm

                    @pl.when(here)
                    def _():
                        pltpu.make_async_copy(source, place, fr.at[x]).start()

                    pl.when(jnp.logical_not(here))(remote.start)

    def finish_blocks(first, count, mixed, matrix):
        flat = jnp.concatenate([dot_t(matrix, part).astype(BF16) for part in mixed], axis=1)
        y_out = dot(flat, wso[...])
        residual = []
        for n in range(count):
            for buffer in (town, trcv):
                residual.append(buffer[first + n].astype(F32).reshape(32, D))
        stream = (jnp.concatenate(residual, axis=0) + y_out).astype(BF16)
        for n in range(count):
            for h in range(2):
                at = (2 * n + h) * 32
                for r in range(4):
                    chunk = (first + n) * 4 + h * 2 + r // 2
                    sbuf[chunk, r % 2] = stream[at + 8 * r : at + 8 * r + 8, :]

    def front(t):
        slot, pair = t % 2, []

        def norm():
            received = normed_pair(trcv, t)
            own_pair = xin[t * 64 : t * 64 + 64, :]
            pair.append(received)
            pair.append(
                jnp.concatenate(
                    [own_pair[:32], received[:32], own_pair[32:], received[32:]], axis=0
                )
            )

        def project(n):
            lanes = slice(n * GROUP, n * GROUP + GROUP)
            qrcv[slot, :, lanes] = dot(pair[0], wsq[:, lanes]).astype(BF16)

        def project_values(n):
            part_rows = slice(n * GROUP, n * GROUP + GROUP)
            values[slot, part_rows, :] = dot_t(wsv[part_rows, :], pair[1]).astype(BF16)

        work = [norm] + [functools.partial(project, n) for n in (0, 3, 1, 4, 2, 5)]
        return work + [functools.partial(project_values, n) for n in range(3)]

    def window(t, w, g):
        own_rows = slice(t * 64 + w * 32, t * 64 + w * 32 + 32)

        def part(n):
            lanes = slice(n * D + g * GROUP, n * D + g * GROUP + GROUP)
            received = qrcv[t % 2, w * 32 : w * 32 + 32, lanes]
            return jnp.concatenate([qown[own_rows, lanes], received], axis=0)

        def store(p, mixed):
            at = (2 * t + w + 1) * 128
            mix[2 * g + p, :, at : at + 128] = mixed

        def group_values():
            return values[t % 2, g * GROUP : g * GROUP + GROUP, :]

        return lambda: part(0), lambda: part(1), group_values, w, store

    for i in range(3):
        z_copy(i).wait_recv()
    for work in front(0):
        work()
    for t in range(4):
        for i in range(2 * t + 3, min(2 * t + 5, 8)):
            z_copy(i).wait_recv()
        bodies = [window(t, w, g) for w in range(2) for g in range(3)]
        attend_all(bodies, None, same_head, front(t + 1) if t < 3 else ())
        recent = [mix[p, :, t * 256 : t * 256 + 384] for p in range(6)]
        finish_blocks(2 * t, 2, recent, scatter)
        if t:
            send_block(2 * t)
        send_block(2 * t + 1)

    edge = [jnp.concatenate([mix[p, :, 1024:1152], mix[p, :, 128:256]], axis=1) for p in range(6)]
    finish_blocks(0, 1, edge, scatter[:64, :256])
    send_block(0)

    loads[2].wait()
    loads[3].wait()
    transpose_values(wtq, wtv)

    rows, cols = iota((128, 128), 0), iota((128, 128), 1)
    regroup = one_hot((rows // 8 == lax.rem(cols, 16)) & (lax.rem(rows, 8) == cols // 16))
    rows, cols = iota((256, 512), 0), iota((256, 512), 1)
    swap = one_hot(
        (rows // 64 == lax.rem(cols // 16, 4))
        & (lax.rem(rows // 8, 8) == lax.rem(cols, 8))
        & (lax.rem(rows, 8) == 2 * (cols // 128) + lax.rem(cols // 8, 2))
    )

    @pl.loop(0, 4)
    def _(n):
        source = lax.rem(x + 3 - n, 4)
        pltpu.make_async_copy(rbuf.at[source], rbuf.at[source], fr.at[source]).wait()
        normed = layer_norm(rbuf[source].astype(F32).reshape(128, D))
        ordered = dot(regroup, normed).astype(BF16)
        normed_t[source] = ordered
        for m in range(6):
            lanes = slice(m * GROUP, m * GROUP + GROUP)
            qt[source, :, lanes] = dot(ordered, wtq[:, lanes]).astype(BF16)

    def at(q, lp):
        return slice(q * 32 + lp * 16, q * 32 + lp * 16 + 16)

    def later(q):
        def project_values(n):
            tokens_pair = jnp.concatenate(
                [normed_t[s, at(q, lp), :] for lp in range(2) for s in range(4)], axis=0
            )
            part_rows = slice(n * GROUP, n * GROUP + GROUP)
            values[q % 2, part_rows, :] = dot_t(wtv[part_rows, :], tokens_pair).astype(BF16)

        return [functools.partial(project_values, n) for n in range(3)]

    def location(q, lp, g):
        def part(n):
            lanes = slice(n * D + g * GROUP, n * D + g * GROUP + GROUP)
            return jnp.concatenate([qt[s, at(q, lp), lanes] for s in range(4)], axis=0)

        def store(p, mixed):
            place = (2 * (q % 2) + lp) * 128
            mixt[q // 2, 2 * g + p, :, place : place + 128] = mixed

        def group_values():
            return values[q % 2, g * GROUP : g * GROUP + GROUP, :]

        return lambda: part(0), lambda: part(1), group_values, lp, store

    def give_back(r):
        for p in range(6):
            xout[:, p * 128 : p * 128 + 128] = dot_t(swap, mixt[r, p]).astype(BF16)
        for n in range(3):
            lanes = slice(n * GROUP, n * GROUP + GROUP)
            branch = dot(xout[...], wto[:, lanes])
            residual = rbuf[:, :, r, :, lanes].astype(F32).reshape(256, GROUP)
            result = (residual + branch).astype(BF16)
            for k in range(32):
                frame = (k % 8) // 2 * 8 + k // 8 * 2 + k % 2
                obuf[r * 32 + frame, :, lanes] = result[k * 8 : k * 8 + 8, :]

        place = out.at[2 * y + r, column]

        @pl.loop(1, 32)
        def _(n):
            target = lax.rem(tm + n, 32)
            pltpu.make_async_remote_copy(
                src_ref=obuf.at[r * 32 + target],
                dst_ref=place,
                send_sem=bs,
                recv_sem=br,
                device_id=(target, z),
                device_id_type=MESH,
            ).start()

        pltpu.make_async_copy(obuf.at[r * 32 + tm], place, br).start()

    for work in later(0):
        work()
    for q in range(4):
        bodies = [location(q, lp, g) for lp in range(2) for g in range(3)]
        attend_all(bodies, mask[...] != 0, same_head, later(q + 1) if q < 3 else ())
        if q % 2:
            give_back(q // 2)

    def wait_bytes(ref, sem):
        pltpu.make_async_copy(ref, ref, sem).wait()

    wait_bytes(out, br)
    wait_bytes(trcv, zs)
    local = y // 2 == 1 - core

    @pl.when(local)
    def _():
        wait_bytes(sbuf.at[pl.ds(0, 31)], fs)

    @pl.when(jnp.logical_not(local))
    def _():
        wait_bytes(sbuf, fs)

    wait_bytes(obuf.at[pl.ds(0, 62)], bs)


def write_out(result, out, sem):
    copy = pltpu.make_async_copy(result, out, sem)
    copy.start()
    copy.wait()


def per_device(
    tokens, col_shift, frame_group, spatial_qkv, spatial_out, temporal_qkv, temporal_out
):
    smem = pl.BlockSpec(memory_space=pltpu.SMEM)
    anywhere = pl.BlockSpec(memory_space=pl.ANY)
    dma = pltpu.SemaphoreType.DMA
    result = pl.pallas_call(
        kernel,
        out_shape=pltpu.VMEM((8, 8, 8, D), BF16),
        in_specs=[smem, smem] + [anywhere] * 5,
        out_specs=pl.BlockSpec(memory_space=pltpu.VMEM),
        scratch_shapes=[
            pltpu.VMEM((D, 3 * D), BF16),
            pltpu.VMEM((D, D), BF16),
            pltpu.VMEM((D, 3 * D), BF16),
            pltpu.VMEM((D, D), BF16),
            pltpu.VMEM((D, D), BF16),
            pltpu.VMEM((D, D), BF16),
            pltpu.VMEM((8, 4, 8, D), BF16),
            pltpu.VMEM((8, 4, 8, D), BF16),
            pltpu.VMEM((256, D), BF16),
            pltpu.VMEM((256, 2 * D), BF16),
            pltpu.VMEM((2, 64, 2 * D), BF16),
            pltpu.VMEM((2, D, 128), BF16),
            pltpu.VMEM((6, 128, 9 * 128), BF16),
            pltpu.VMEM((32, 2, 8, D), BF16),
            pltpu.VMEM((4, 8, 2, 8, D), BF16),
            pltpu.VMEM((4, 128, D), BF16),
            pltpu.VMEM((4, 128, 2 * D), BF16),
            pltpu.VMEM((2, 6, 128, 512), BF16),
            pltpu.VMEM((256, D), BF16),
            pltpu.VMEM((64, 8, D), BF16),
            pltpu.VMEM((64, GROUP), jnp.int32),
            dma((4,)),
            dma((8,)),
            dma,
            dma((8,)),
            dma,
            dma((4,)),
            dma,
            dma,
        ],
        compiler_params=pltpu.CompilerParams(
            collective_id=0, has_side_effects=True, vmem_limit_bytes=56 * 1024 * 1024
        ),
    )(
        col_shift,
        frame_group,
        tokens.reshape(8, 8, 8, D),
        spatial_qkv,
        spatial_out,
        temporal_qkv,
        temporal_out,
    )
    written = pl.pallas_call(
        write_out,
        out_shape=jax.ShapeDtypeStruct((8, 8, 8, D), BF16),
        in_specs=[anywhere],
        out_specs=anywhere,
        scratch_shapes=[dma],
    )(pltpu.with_memory_space_constraint(result, pltpu.VMEM))
    return written.reshape(tokens.shape)


def solution(mesh):
    in_specs = (P("tm", "rows", None, None), P("tm"), P(), P(), P(), P(), P())
    out_specs = P("tm", "rows", None, None)
    return jax.shard_map(
        per_device, mesh=mesh, in_specs=in_specs, out_specs=out_specs, check_vma=False
    )
```

```python
import functools

import jax
import jax.numpy as jnp
from jax import lax
from jax.experimental import pallas as pl
from jax.experimental.pallas import tpu as pltpu
from jax.sharding import PartitionSpec as P

D = 768
GROUP = 256
BF16 = jnp.bfloat16
F32 = jnp.float32
MESH = pl.DeviceIdType.MESH
AHEAD = 2
BEHIND = 2


def iota(shape, dim):
    return lax.broadcasted_iota(jnp.int32, shape, dim)


def one_hot(mask):
    return jnp.where(mask, 1.0, 0.0).astype(BF16)


def layer_norm(x):
    center = x - jnp.mean(x, axis=-1, keepdims=True)
    spread = jnp.mean(center * center, axis=-1, keepdims=True)
    return (center * lax.rsqrt(spread + 1e-05)).astype(BF16)


def dot(a, b):
    return jnp.dot(a, b, preferred_element_type=F32)


def dot_t(a, b):
    return lax.dot_general(a, b, (((1,), (1,)), ((), ())), preferred_element_type=F32)


def block_diagonal(x):
    lane = iota(x.shape, 1) // 64
    return jnp.concatenate([jnp.where(lane == h, x, jnp.zeros_like(x)) for h in range(4)], axis=0)


def attend(s):
    e = jnp.exp((s - jnp.max(s, axis=0, keepdims=True)) * 0.125)
    return (e * (1.0 / jnp.sum(e, axis=0, keepdims=True))).astype(BF16)


def attend_all(bodies, allowed, same_head, extra=()):
    extra = list(extra)
    share = -(-len(extra) // len(bodies))
    def scores(body):
        s = dot_t(body[1](), block_diagonal(body[0]()))
        return s if allowed is None else jnp.where(allowed, s, -1e30)

    waiting, ready = [scores(body) for body in bodies[:AHEAD]], []
    for n, body in enumerate(bodies):
        if n + AHEAD < len(bodies):
            waiting.append(scores(bodies[n + AHEAD]))
        ready.append(attend(waiting[n]))
        if n >= BEHIND:
            mix_values(ready[n - BEHIND], *bodies[n - BEHIND][2:], same_head)
        for work in extra[n * share : n * share + share]:
            work()
    for n in range(len(bodies) - BEHIND, len(bodies)):
        mix_values(ready[n], *bodies[n][2:], same_head)


def mix_values(weights, values, slot, store, same_head):
    values = values()
    blank = jnp.zeros_like(weights)
    padded = jnp.concatenate([blank, weights] if slot else [weights, blank], axis=0)
    for p in range(2):
        lanes = slice(p * 128, p * 128 + 128)
        mixed = dot(values[lanes, :], padded[:, lanes])
        store(p, jnp.where(same_head, mixed, 0.0).astype(BF16))


def kernel(
    shift_ref, group_ref, tok, wsq_h, wso_h, wtq_h, wto_h, out,
    wsq, wso, wtq, wto, wsv, wtv, town, trcv, xin, qown, qrcv, values, mix, sbuf, rbuf, normed_t, qt,
    mixt, xout, obuf, mask, lsem, osem, zs, zr, fs, fr, bs, br,
):
    tm = lax.axis_index("tm")
    z = lax.axis_index("rows")
    core = lax.rem(tm, 2)
    x = lax.rem(tm // 2, 4)
    y = tm // 8
    zup = lax.rem(z + 1 + 6 * core, 8)
    zdown = lax.rem(z + 7 + 2 * core, 8)

    loads = [
        pltpu.make_async_copy(src, dst, lsem.at[n])
        for n, (src, dst) in enumerate(((wsq_h, wsq), (wso_h, wso), (wtq_h, wtq), (wto_h, wto)))
    ]

    def own_copy(i):
        return pltpu.make_async_copy(
            tok.at[pl.ds(4 - 4 * core, 4), i], town.at[i], osem.at[i]
        )

    @pl.loop(0, 8)
    def _(i):
        own_copy(i).start()

    loads[0].start()
    loads[1].start()

    barrier = pltpu.get_barrier_semaphore()
    pl.semaphore_signal(barrier, inc=1, device_id=(tm, zup), device_id_type=MESH)

    @pl.loop(1, 32)
    def _(n):
        pl.semaphore_signal(
            barrier, inc=1, device_id=(lax.rem(tm + n, 32), z), device_id_type=MESH
        )

    sender_core = y // 2
    sender_z = lax.rem(z + 7 + 2 * sender_core, 8)

    @pl.loop(0, 16)
    def _(n):
        pl.semaphore_signal(
            barrier, inc=1, device_id=(2 * n + sender_core, sender_z), device_id_type=MESH
        )

    shift = shift_ref[0]

    rows, cols = iota((64, 96), 0), iota((64, 96), 1)
    gather = one_hot(
        (lax.rem(rows // 8, 4) == lax.rem(cols // 8, 4))
        & (8 * (cols // 32) + lax.rem(cols, 8) == 8 * (rows // 32) + lax.rem(rows, 8) + shift)
    )
    rows, cols = iota((128, 384), 0), iota((128, 384), 1)
    scatter = one_hot(
        (lax.rem(rows // 8, 8) == lax.rem(cols // 8, 8))
        & (8 * (rows // 64) + lax.rem(rows, 8) + 8 == 8 * (cols // 128) + lax.rem(cols, 8) + shift)
    )
    same_head = iota((128, 128), 0) // 64 == iota((128, 128), 1) // 64
    unit = one_hot(iota((GROUP, GROUP), 0) == iota((GROUP, GROUP), 1))

    def transpose_values(weight, result, i):
        rows_out = slice(i * GROUP, i * GROUP + GROUP)
        lanes = slice(2 * D + i * GROUP, 2 * D + i * GROUP + GROUP)
        for j in range(3):
            part = slice(j * GROUP, j * GROUP + GROUP)
            result[rows_out, part] = dot_t(unit, weight[part, lanes]).astype(BF16)

    def normed_pair(buffer, t):
        parts = []
        for b in range(3):
            parts.append(buffer[(2 * t + b) % 8 if isinstance(t, int) else lax.rem(2 * t + b, 8)].astype(F32).reshape(32, D))
        normed = layer_norm(jnp.concatenate(parts, axis=0))
        return dot(gather, normed).astype(BF16)

    @pl.loop(0, 8)
    def _(i):
        own_copy(i).wait()

    @pl.loop(0, 4)
    def _(t):
        xin[pl.ds(pl.multiple_of(t * 64, 64), 64), :] = normed_pair(town, t)

    pl.semaphore_wait(barrier, 48)

    def z_copy(i):
        return pltpu.make_async_remote_copy(
            src_ref=tok.at[pl.ds(4 * core, 4), i],
            dst_ref=trcv.at[i],
            send_sem=zs,
            recv_sem=zr.at[i],
            device_id=(tm, zdown),
            device_id_type=MESH,
        )

    @pl.loop(0, 8)
    def _(i):
        z_copy(i).start()

    loads[0].wait()
    loads[2].start()
    loads[3].start()

    def project_own(n):
        lanes = pl.ds(pl.multiple_of(n * GROUP, GROUP), GROUP)
        qown[:, lanes] = dot(xin[...], wsq[:, lanes]).astype(BF16)

    pl.loop(0, 6)(project_own)
    for i in range(3):
        transpose_values(wsq, wsv, i)

    for p in range(6):
        mix[p, :, 0:128] = jnp.zeros((128, 128), BF16)

    k_row, q_col = iota((64, 1), 0), lax.rem(iota((1, GROUP), 1), 64)

    def frame_of(n):
        m = lax.rem(n, 8)
        return (m // 2) * 8 + (n // 16) * 2 + lax.rem(m, 2)

    k_frame, q_frame = frame_of(k_row), frame_of(q_col)
    q_group, k_group = jnp.zeros_like(q_frame), jnp.zeros_like(k_frame)
    for f in range(32):
        value = group_ref[f]
        q_group = jnp.where(q_frame == f, value, q_group)
        k_group = jnp.where(k_frame == f, value, k_group)
    same = lax.rem(k_row // 8, 2) == lax.rem(q_col // 8, 2)
    mask[...] = jnp.where(same & (k_group <= q_group), 1, 0)

    loads[1].wait()

    own_row = 2 * y + x // 2

    def send_block(i):
        number = (i + 7) % 8
        r, side, low = number // 4, number // 2 % 2, number % 2
        place = rbuf.at[r, x, 2 * y + core]

        def send(h, row):
            half = core if h else 1 - core
            p = 4 * half + row
            target = ((p // 2) * 4 + 2 * lax.rem(p, 2) + low) * 2 + side
            return pltpu.make_async_remote_copy(
                src_ref=sbuf.at[i * 8 + h * 4 + row],
                dst_ref=place,
                send_sem=fs,
                recv_sem=fr.at[r],
                device_id=(target, zup if h else z),
                device_id_type=MESH,
            )

        for row in range(4):
            send(1, row).start()
        mine = lax.rem(own_row, 4)
        for n in range(1, 4):
            send(0, lax.rem(mine + n, 4)).start()
        here = (y // 2 == 1 - core) & (core == side) & (lax.rem(x, 2) == low)

        @pl.when(here)
        def _():
            pltpu.make_async_copy(sbuf.at[i * 8 + mine], place, fr.at[r]).start()

        @pl.when(jnp.logical_not(here))
        def _():
            send(0, mine).start()

    def finish_blocks(first, count, mixed, matrix):
        flat = jnp.concatenate([dot_t(matrix, part).astype(BF16) for part in mixed], axis=1)
        y_out = dot(flat, wso[...])
        residual = []
        for n in range(count):
            for buffer in (town, trcv):
                residual.append(buffer[first + n].astype(F32).reshape(32, D))
        stream = (jnp.concatenate(residual, axis=0) + y_out).astype(BF16)
        for n in range(count):
            for h in range(2):
                at = (2 * n + h) * 32
                for r in range(4):
                    sbuf[(first + n) * 8 + h * 4 + r] = stream[at + 8 * r : at + 8 * r + 8, :]

    def front(t):
        slot, pair = t % 2, []

        def norm():
            received = normed_pair(trcv, t)
            own_pair = xin[t * 64 : t * 64 + 64, :]
            pair.append(received)
            pair.append(
                jnp.concatenate(
                    [own_pair[:32], received[:32], own_pair[32:], received[32:]], axis=0
                )
            )

        def project(n):
            lanes = slice(n * GROUP, n * GROUP + GROUP)
            qrcv[slot, :, lanes] = dot(pair[0], wsq[:, lanes]).astype(BF16)

        def project_values(n):
            part_rows = slice(n * GROUP, n * GROUP + GROUP)
            values[slot, part_rows, :] = dot_t(wsv[part_rows, :], pair[1]).astype(BF16)

        work = [norm] + [functools.partial(project, n) for n in (0, 3, 1, 4, 2, 5)]
        return work + [functools.partial(project_values, n) for n in range(3)]

    def window(t, w, g):
        own_rows = slice(t * 64 + w * 32, t * 64 + w * 32 + 32)

        def part(n):
            lanes = slice(n * D + g * GROUP, n * D + g * GROUP + GROUP)
            received = qrcv[t % 2, w * 32 : w * 32 + 32, lanes]
            return jnp.concatenate([qown[own_rows, lanes], received], axis=0)

        def store(p, mixed):
            at = (2 * t + w + 1) * 128
            mix[2 * g + p, :, at : at + 128] = mixed

        def group_values():
            return values[t % 2, g * GROUP : g * GROUP + GROUP, :]

        return lambda: part(0), lambda: part(1), group_values, w, store

    for i in range(3):
        z_copy(i).wait_recv()
    for work in front(0):
        work()
    for t in range(4):
        for i in range(2 * t + 3, min(2 * t + 5, 8)):
            z_copy(i).wait_recv()
        bodies = [window(t, w, g) for w in range(2) for g in range(3)]
        if t < 3:
            extra = front(t + 1)
        else:
            loads[2].wait()
            extra = [functools.partial(transpose_values, wtq, wtv, i) for i in range(3)]
        attend_all(bodies, None, same_head, extra)
        recent = [mix[p, :, t * 256 : t * 256 + 384] for p in range(6)]
        finish_blocks(2 * t, 2, recent, scatter)
        if t:
            send_block(2 * t)
        send_block(2 * t + 1)

    edge = [jnp.concatenate([mix[p, :, 1024:1152], mix[p, :, 128:256]], axis=1) for p in range(6)]
    finish_blocks(0, 1, edge, scatter[:64, :256])
    send_block(0)

    loads[3].wait()
    rows, cols = iota((256, 256), 0), iota((256, 256), 1)
    regroup = one_hot(
        (rows // 64 == cols // 64)
        & (lax.rem(rows // 8, 8) == lax.rem(cols, 8))
        & (lax.rem(rows, 8) == lax.rem(cols // 8, 8))
    )
    rows, cols = iota((256, 512), 0), iota((256, 512), 1)
    swap = one_hot(
        (rows // 64 == lax.rem(cols // 16, 4))
        & (lax.rem(rows // 8, 8) == lax.rem(cols, 8))
        & (lax.rem(rows, 8) == 2 * (cols // 128) + lax.rem(cols // 8, 2))
    )

    def wait_bytes(ref, sem):
        pltpu.make_async_copy(ref, ref, sem).wait()

    def project_half(r):
        wait_bytes(rbuf.at[r], fr.at[r])
        normed = layer_norm(rbuf[r].astype(F32).reshape(256, D))
        normed_t[r] = dot(regroup, normed).astype(BF16)
        for m in range(6):
            lanes = slice(m * GROUP, m * GROUP + GROUP)
            qt[r, :, lanes] = dot(normed_t[r], wtq[:, lanes]).astype(BF16)

    def at(q, lp, s):
        first = s * 64 + q % 2 * 32 + lp * 16
        return slice(first, first + 16)

    def later(q):
        def project_values(n):
            tokens_pair = jnp.concatenate(
                [normed_t[q // 2, at(q, lp, s), :] for lp in range(2) for s in range(4)], axis=0
            )
            part_rows = slice(n * GROUP, n * GROUP + GROUP)
            values[q % 2, part_rows, :] = dot_t(wtv[part_rows, :], tokens_pair).astype(BF16)

        return [functools.partial(project_values, n) for n in range(3)]

    def location(q, lp, g):
        def part(n):
            lanes = slice(n * D + g * GROUP, n * D + g * GROUP + GROUP)
            return jnp.concatenate([qt[q // 2, at(q, lp, s), lanes] for s in range(4)], axis=0)

        def store(p, mixed):
            place = (2 * (q % 2) + lp) * 128
            mixt[q // 2, 2 * g + p, :, place : place + 128] = mixed

        def group_values():
            return values[q % 2, g * GROUP : g * GROUP + GROUP, :]

        return lambda: part(0), lambda: part(1), group_values, lp, store

    def give_back(r):
        for p in range(6):
            xout[:, p * 128 : p * 128 + 128] = dot_t(swap, mixt[r, p]).astype(BF16)
        for n in range(3):
            lanes = slice(n * GROUP, n * GROUP + GROUP)
            branch = dot(xout[...], wto[:, lanes])
            residual = rbuf[r, :, :, :, lanes].astype(F32).reshape(256, GROUP)
            result = (residual + branch).astype(BF16)
            for k in range(32):
                frame = (k % 8) // 2 * 8 + k // 8 * 2 + k % 2
                obuf[r * 32 + frame, :, lanes] = result[k * 8 : k * 8 + 8, :]

        place = out.at[own_row, lax.rem(r * 4 + core * 2 + lax.rem(x, 2) + 1, 8)]

        @pl.loop(1, 32)
        def _(n):
            target = lax.rem(tm + n, 32)
            pltpu.make_async_remote_copy(
                src_ref=obuf.at[r * 32 + target],
                dst_ref=place,
                send_sem=bs,
                recv_sem=br,
                device_id=(target, z),
                device_id_type=MESH,
            ).start()

        pltpu.make_async_copy(obuf.at[r * 32 + tm], place, br).start()

    for q in range(4):
        if q % 2 == 0:
            project_half(q // 2)
            for work in later(q):
                work()
        bodies = [location(q, lp, g) for lp in range(2) for g in range(3)]
        attend_all(bodies, mask[...] != 0, same_head, () if q % 2 else later(q + 1))
        if q % 2:
            give_back(q // 2)

    wait_bytes(out, br)
    wait_bytes(trcv, zs)
    local = y // 2 == 1 - core

    @pl.when(local)
    def _():
        wait_bytes(sbuf.at[pl.ds(0, 62)], fs)

    @pl.when(jnp.logical_not(local))
    def _():
        wait_bytes(sbuf, fs)

    wait_bytes(obuf.at[pl.ds(0, 62)], bs)


def write_out(result, out, sem):
    copy = pltpu.make_async_copy(result, out, sem)
    copy.start()
    copy.wait()


def per_device(
    tokens, col_shift, frame_group, spatial_qkv, spatial_out, temporal_qkv, temporal_out
):
    smem = pl.BlockSpec(memory_space=pltpu.SMEM)
    anywhere = pl.BlockSpec(memory_space=pl.ANY)
    dma = pltpu.SemaphoreType.DMA
    result = pl.pallas_call(
        kernel,
        out_shape=pltpu.VMEM((8, 8, 8, D), BF16),
        in_specs=[smem, smem] + [anywhere] * 5,
        out_specs=pl.BlockSpec(memory_space=pltpu.VMEM),
        scratch_shapes=[
            pltpu.VMEM((D, 3 * D), BF16),
            pltpu.VMEM((D, D), BF16),
            pltpu.VMEM((D, 3 * D), BF16),
            pltpu.VMEM((D, D), BF16),
            pltpu.VMEM((D, D), BF16),
            pltpu.VMEM((D, D), BF16),
            pltpu.VMEM((8, 4, 8, D), BF16),
            pltpu.VMEM((8, 4, 8, D), BF16),
            pltpu.VMEM((256, D), BF16),
            pltpu.VMEM((256, 2 * D), BF16),
            pltpu.VMEM((2, 64, 2 * D), BF16),
            pltpu.VMEM((2, D, 128), BF16),
            pltpu.VMEM((6, 128, 9 * 128), BF16),
            pltpu.VMEM((64, 8, D), BF16),
            pltpu.VMEM((2, 4, 8, 8, D), BF16),
            pltpu.VMEM((2, 256, D), BF16),
            pltpu.VMEM((2, 256, 2 * D), BF16),
            pltpu.VMEM((2, 6, 128, 512), BF16),
            pltpu.VMEM((256, D), BF16),
            pltpu.VMEM((64, 8, D), BF16),
            pltpu.VMEM((64, GROUP), jnp.int32),
            dma((4,)),
            dma((8,)),
            dma,
            dma((8,)),
            dma,
            dma((2,)),
            dma,
            dma,
        ],
        compiler_params=pltpu.CompilerParams(
            collective_id=0, has_side_effects=True, vmem_limit_bytes=56 * 1024 * 1024
        ),
    )(
        col_shift,
        frame_group,
        tokens.reshape(8, 8, 8, D),
        spatial_qkv,
        spatial_out,
        temporal_qkv,
        temporal_out,
    )
    written = pl.pallas_call(
        write_out,
        out_shape=jax.ShapeDtypeStruct((8, 8, 8, D), BF16),
        in_specs=[anywhere],
        out_specs=anywhere,
        scratch_shapes=[dma],
    )(pltpu.with_memory_space_constraint(result, pltpu.VMEM))
    return written.reshape(tokens.shape)


def solution(mesh):
    in_specs = (P("tm", "rows", None, None), P("tm"), P(), P(), P(), P(), P())
    out_specs = P("tm", "rows", None, None)
    return jax.shard_map(
        per_device, mesh=mesh, in_specs=in_specs, out_specs=out_specs, check_vma=False
    )
```

```python
import functools

import jax
import jax.numpy as jnp
from jax import lax
from jax.experimental import pallas as pl
from jax.experimental.pallas import tpu as pltpu
from jax.sharding import PartitionSpec as P

D = 768
GROUP = 256
BF16 = jnp.bfloat16
F32 = jnp.float32
MESH = pl.DeviceIdType.MESH
AHEAD = 2
BEHIND = 2
FAR_FIRST = [(dy, dx, dc) for dy in (2, 1, 3, 0) for dx in (2, 1, 3, 0) for dc in (0, 1)]
FAR_FIRST.remove((0, 0, 0))
FAR_FIRST.sort(key=lambda d: -min(d[0], 4 - d[0]) - min(d[1], 4 - d[1]))


def iota(shape, dim):
    return lax.broadcasted_iota(jnp.int32, shape, dim)


def one_hot(mask):
    return jnp.where(mask, 1.0, 0.0).astype(BF16)


def layer_norm(x):
    center = x - jnp.mean(x, axis=-1, keepdims=True)
    spread = jnp.mean(center * center, axis=-1, keepdims=True)
    return (center * lax.rsqrt(spread + 1e-05)).astype(BF16)


def dot(a, b):
    return jnp.dot(a, b, preferred_element_type=F32)


def dot_t(a, b):
    return lax.dot_general(a, b, (((1,), (1,)), ((), ())), preferred_element_type=F32)


def block_diagonal(x):
    lane = iota(x.shape, 1) // 64
    return jnp.concatenate([jnp.where(lane == h, x, jnp.zeros_like(x)) for h in range(4)], axis=0)


def attend(s):
    e = jnp.exp((s - jnp.max(s, axis=0, keepdims=True)) * 0.125)
    return (e * (1.0 / jnp.sum(e, axis=0, keepdims=True))).astype(BF16)


def attend_all(bodies, allowed, same_head, extra=()):
    extra = list(extra)
    share = -(-len(extra) // len(bodies))
    def scores(body):
        s = dot_t(body[1](), block_diagonal(body[0]()))
        return s if allowed is None else jnp.where(allowed, s, -1e30)

    waiting, ready = [scores(body) for body in bodies[:AHEAD]], []
    for n, body in enumerate(bodies):
        if n + AHEAD < len(bodies):
            waiting.append(scores(bodies[n + AHEAD]))
        ready.append(attend(waiting[n]))
        if n >= BEHIND:
            mix_values(ready[n - BEHIND], *bodies[n - BEHIND][2:], same_head)
        for work in extra[n * share : n * share + share]:
            work()
    for n in range(len(bodies) - BEHIND, len(bodies)):
        mix_values(ready[n], *bodies[n][2:], same_head)


def mix_values(weights, values, slot, store, same_head):
    values = values()
    blank = jnp.zeros_like(weights)
    padded = jnp.concatenate([blank, weights] if slot else [weights, blank], axis=0)
    for p in range(2):
        lanes = slice(p * 128, p * 128 + 128)
        mixed = dot(values[lanes, :], padded[:, lanes])
        store(p, jnp.where(same_head, mixed, 0.0).astype(BF16))


def kernel(
    shift_ref, group_ref, tok, wsq_h, wso_h, wtq_h, wto_h, out,
    wsq, wso, wtq, wto, wsv, wtv, town, trcv, xin, qown, qrcv, values, mix, sbuf, rbuf, normed_t, qt,
    mixt, xout, obuf, mask, lsem, osem, zs, zr, fs, fr, bs, br,
):
    tm = lax.axis_index("tm")
    z = lax.axis_index("rows")
    core = lax.rem(tm, 2)
    x = lax.rem(tm // 2, 4)
    y = tm // 8
    zup = lax.rem(z + 1 + 6 * core, 8)
    zdown = lax.rem(z + 7 + 2 * core, 8)

    barrier = pltpu.get_barrier_semaphore()
    pl.semaphore_signal(barrier, inc=1, device_id=(tm, zup), device_id_type=MESH)

    loads = [
        pltpu.make_async_copy(src, dst, lsem.at[n])
        for n, (src, dst) in enumerate(((wsq_h, wsq), (wso_h, wso), (wtq_h, wtq), (wto_h, wto)))
    ]

    def own_copy(i):
        return pltpu.make_async_copy(
            tok.at[pl.ds(4 - 4 * core, 4), i], town.at[i], osem.at[i]
        )

    @pl.loop(0, 8)
    def _(i):
        own_copy(i).start()

    loads[0].start()

    @pl.loop(1, 32)
    def _(n):
        pl.semaphore_signal(
            barrier, inc=1, device_id=(lax.rem(tm + n, 32), z), device_id_type=MESH
        )

    sender_core = y // 2
    sender_z = lax.rem(z + 7 + 2 * sender_core, 8)

    @pl.loop(0, 16)
    def _(n):
        pl.semaphore_signal(
            barrier, inc=1, device_id=(2 * n + sender_core, sender_z), device_id_type=MESH
        )

    shift = shift_ref[0]

    rows, cols = iota((64, 96), 0), iota((64, 96), 1)
    gather = one_hot(
        (lax.rem(rows // 8, 4) == lax.rem(cols // 8, 4))
        & (8 * (cols // 32) + lax.rem(cols, 8) == 8 * (rows // 32) + lax.rem(rows, 8) + shift)
    )
    rows, cols = iota((128, 384), 0), iota((128, 384), 1)
    scatter = one_hot(
        (lax.rem(rows // 8, 8) == lax.rem(cols // 8, 8))
        & (8 * (rows // 64) + lax.rem(rows, 8) + 8 == 8 * (cols // 128) + lax.rem(cols, 8) + shift)
    )
    same_head = iota((128, 128), 0) // 64 == iota((128, 128), 1) // 64
    unit = one_hot(iota((GROUP, GROUP), 0) == iota((GROUP, GROUP), 1))

    def transpose_values(weight, result, i):
        rows_out = slice(i * GROUP, i * GROUP + GROUP)
        lanes = slice(2 * D + i * GROUP, 2 * D + i * GROUP + GROUP)
        for j in range(3):
            part = slice(j * GROUP, j * GROUP + GROUP)
            result[rows_out, part] = dot_t(unit, weight[part, lanes]).astype(BF16)

    def normed_pair(buffer, t):
        parts = []
        for b in range(3):
            parts.append(buffer[(2 * t + b) % 8 if isinstance(t, int) else lax.rem(2 * t + b, 8)].astype(F32).reshape(32, D))
        normed = layer_norm(jnp.concatenate(parts, axis=0))
        return dot(gather, normed).astype(BF16)

    @pl.loop(0, 8)
    def _(i):
        own_copy(i).wait()

    @pl.loop(0, 4)
    def _(t):
        xin[pl.ds(pl.multiple_of(t * 64, 64), 64), :] = normed_pair(town, t)

    pl.semaphore_wait(barrier, 48)

    def z_copy(i):
        return pltpu.make_async_remote_copy(
            src_ref=tok.at[pl.ds(4 * core, 4), i],
            dst_ref=trcv.at[i],
            send_sem=zs,
            recv_sem=zr.at[i],
            device_id=(tm, zdown),
            device_id_type=MESH,
        )

    @pl.loop(0, 8)
    def _(i):
        z_copy(i).start()

    loads[0].wait()
    for load in loads[1:]:
        load.start()

    def project_own(n):
        lanes = pl.ds(pl.multiple_of(n * GROUP, GROUP), GROUP)
        qown[:, lanes] = dot(xin[...], wsq[:, lanes]).astype(BF16)

    pl.loop(0, 6)(project_own)
    for i in range(3):
        transpose_values(wsq, wsv, i)

    for p in range(6):
        mix[p, :, 0:128] = jnp.zeros((128, 128), BF16)

    def build_mask():
        k_row, q_col = iota((64, 1), 0), lax.rem(iota((1, GROUP), 1), 64)

        def frame_of(n):
            m = lax.rem(n, 8)
            return (m // 2) * 8 + (n // 16) * 2 + lax.rem(m, 2)

        k_frame, q_frame = frame_of(k_row), frame_of(q_col)
        q_group, k_group = jnp.zeros_like(q_frame), jnp.zeros_like(k_frame)
        for f in range(32):
            value = group_ref[f]
            q_group = jnp.where(q_frame == f, value, q_group)
            k_group = jnp.where(k_frame == f, value, k_group)
        same = lax.rem(k_row // 8, 2) == lax.rem(q_col // 8, 2)
        mask[...] = jnp.where(same & (k_group <= q_group), 1, 0)

    loads[1].wait()

    own_row = 2 * y + x // 2

    def send_block(i):
        number = (i + 7) % 8
        r, side, low = number // 4, number // 2 % 2, number % 2
        place = rbuf.at[r, x, 2 * y + core]

        def send(h, row):
            half = core if h else 1 - core
            p = 4 * half + row
            target = ((p // 2) * 4 + 2 * lax.rem(p, 2) + low) * 2 + side
            return pltpu.make_async_remote_copy(
                src_ref=sbuf.at[i * 8 + h * 4 + row],
                dst_ref=place,
                send_sem=fs,
                recv_sem=fr.at[r],
                device_id=(target, zup if h else z),
                device_id_type=MESH,
            )

        for row in range(4):
            send(1, row).start()
        mine = lax.rem(own_row, 4)
        for n in range(1, 4):
            send(0, lax.rem(mine + n, 4)).start()
        here = (y // 2 == 1 - core) & (core == side) & (lax.rem(x, 2) == low)

        @pl.when(here)
        def _():
            pltpu.make_async_copy(sbuf.at[i * 8 + mine], place, fr.at[r]).start()

        @pl.when(jnp.logical_not(here))
        def _():
            send(0, mine).start()

    def finish_blocks(first, count, mixed, matrix):
        flat = jnp.concatenate([dot_t(matrix, part).astype(BF16) for part in mixed], axis=1)
        y_out = dot(flat, wso[...])
        residual = []
        for n in range(count):
            for buffer in (town, trcv):
                residual.append(buffer[first + n].astype(F32).reshape(32, D))
        stream = (jnp.concatenate(residual, axis=0) + y_out).astype(BF16)
        for n in range(count):
            for h in range(2):
                at = (2 * n + h) * 32
                for r in range(4):
                    sbuf[(first + n) * 8 + h * 4 + r] = stream[at + 8 * r : at + 8 * r + 8, :]

    def front(t):
        slot, pair = t % 2, []

        def norm():
            received = normed_pair(trcv, t)
            own_pair = xin[t * 64 : t * 64 + 64, :]
            pair.append(received)
            pair.append(
                jnp.concatenate(
                    [own_pair[:32], received[:32], own_pair[32:], received[32:]], axis=0
                )
            )

        def project(n):
            lanes = slice(n * GROUP, n * GROUP + GROUP)
            qrcv[slot, :, lanes] = dot(pair[0], wsq[:, lanes]).astype(BF16)

        def project_values(n):
            part_rows = slice(n * GROUP, n * GROUP + GROUP)
            values[slot, part_rows, :] = dot_t(wsv[part_rows, :], pair[1]).astype(BF16)

        work = [norm] + [functools.partial(project, n) for n in (0, 3, 1, 4, 2, 5)]
        return work + [functools.partial(project_values, n) for n in range(3)]

    def window(t, w, g):
        own_rows = slice(t * 64 + w * 32, t * 64 + w * 32 + 32)

        def part(n):
            lanes = slice(n * D + g * GROUP, n * D + g * GROUP + GROUP)
            received = qrcv[t % 2, w * 32 : w * 32 + 32, lanes]
            return jnp.concatenate([qown[own_rows, lanes], received], axis=0)

        def store(p, mixed):
            at = (2 * t + w + 1) * 128
            mix[2 * g + p, :, at : at + 128] = mixed

        def group_values():
            return values[t % 2, g * GROUP : g * GROUP + GROUP, :]

        return lambda: part(0), lambda: part(1), group_values, w, store

    for i in range(3):
        z_copy(i).wait_recv()
    for work in front(0):
        work()
    for t in range(4):
        for i in range(2 * t + 3, min(2 * t + 5, 8)):
            z_copy(i).wait_recv()
        bodies = [window(t, w, g) for w in range(2) for g in range(3)]
        if t < 3:
            extra = front(t + 1)
        else:
            loads[2].wait()
            extra = [functools.partial(transpose_values, wtq, wtv, i) for i in range(3)]
            extra.append(build_mask)
        attend_all(bodies, None, same_head, extra)
        recent = [mix[p, :, t * 256 : t * 256 + 384] for p in range(6)]
        finish_blocks(2 * t, 2, recent, scatter)
        if t:
            send_block(2 * t)
        send_block(2 * t + 1)

    edge = [jnp.concatenate([mix[p, :, 1024:1152], mix[p, :, 128:256]], axis=1) for p in range(6)]
    finish_blocks(0, 1, edge, scatter[:64, :256])
    send_block(0)

    loads[3].wait()
    rows, cols = iota((256, 256), 0), iota((256, 256), 1)
    regroup = one_hot(
        (rows // 64 == cols // 64)
        & (lax.rem(rows // 8, 8) == lax.rem(cols, 8))
        & (lax.rem(rows, 8) == lax.rem(cols // 8, 8))
    )
    rows, cols = iota((256, 512), 0), iota((256, 512), 1)
    swap = one_hot(
        (rows // 64 == lax.rem(cols // 16, 4))
        & (lax.rem(rows // 8, 8) == lax.rem(cols, 8))
        & (lax.rem(rows, 8) == 2 * (cols // 128) + lax.rem(cols // 8, 2))
    )

    def wait_bytes(ref, sem):
        pltpu.make_async_copy(ref, ref, sem).wait()

    def project_half(r):
        wait_bytes(rbuf.at[r], fr.at[r])
        normed = layer_norm(rbuf[r].astype(F32).reshape(256, D))
        normed_t[r] = dot(regroup, normed).astype(BF16)
        for m in range(6):
            lanes = slice(m * GROUP, m * GROUP + GROUP)
            qt[r, :, lanes] = dot(normed_t[r], wtq[:, lanes]).astype(BF16)

    def at(q, lp, s):
        first = s * 64 + q % 2 * 32 + lp * 16
        return slice(first, first + 16)

    def later(q):
        def project_values(n):
            tokens_pair = jnp.concatenate(
                [normed_t[q // 2, at(q, lp, s), :] for lp in range(2) for s in range(4)], axis=0
            )
            part_rows = slice(n * GROUP, n * GROUP + GROUP)
            values[q % 2, part_rows, :] = dot_t(wtv[part_rows, :], tokens_pair).astype(BF16)

        return [functools.partial(project_values, n) for n in range(3)]

    def location(q, lp, g):
        def part(n):
            lanes = slice(n * D + g * GROUP, n * D + g * GROUP + GROUP)
            return jnp.concatenate([qt[q // 2, at(q, lp, s), lanes] for s in range(4)], axis=0)

        def store(p, mixed):
            place = (2 * (q % 2) + lp) * 128
            mixt[q // 2, 2 * g + p, :, place : place + 128] = mixed

        def group_values():
            return values[q % 2, g * GROUP : g * GROUP + GROUP, :]

        return lambda: part(0), lambda: part(1), group_values, lp, store

    def give_back(r):
        for p in range(6):
            xout[:, p * 128 : p * 128 + 128] = dot_t(swap, mixt[r, p]).astype(BF16)
        for n in range(3):
            lanes = slice(n * GROUP, n * GROUP + GROUP)
            branch = dot(xout[...], wto[:, lanes])
            residual = rbuf[r, :, :, :, lanes].astype(F32).reshape(256, GROUP)
            result = (residual + branch).astype(BF16)
            for k in range(32):
                frame = (k % 8) // 2 * 8 + k // 8 * 2 + k % 2
                obuf[r * 32 + frame, :, lanes] = result[k * 8 : k * 8 + 8, :]

        place = out.at[own_row, lax.rem(r * 4 + core * 2 + lax.rem(x, 2) + 1, 8)]

        for dy, dx, dc in FAR_FIRST:
            target = (lax.rem(y + dy, 4) * 4 + lax.rem(x + dx, 4)) * 2 + lax.rem(core + dc, 2)
            pltpu.make_async_remote_copy(
                src_ref=obuf.at[r * 32 + target],
                dst_ref=place,
                send_sem=bs,
                recv_sem=br,
                device_id=(target, z),
                device_id_type=MESH,
            ).start()

        pltpu.make_async_copy(obuf.at[r * 32 + tm], place, br).start()

    for q in range(4):
        if q % 2 == 0:
            project_half(q // 2)
            for work in later(q):
                work()
        bodies = [location(q, lp, g) for lp in range(2) for g in range(3)]
        attend_all(bodies, mask[...] != 0, same_head, () if q % 2 else later(q + 1))
        if q % 2:
            give_back(q // 2)

    wait_bytes(out, br)
    wait_bytes(trcv, zs)
    local = y // 2 == 1 - core

    @pl.when(local)
    def _():
        wait_bytes(sbuf.at[pl.ds(0, 62)], fs)

    @pl.when(jnp.logical_not(local))
    def _():
        wait_bytes(sbuf, fs)

    wait_bytes(obuf.at[pl.ds(0, 62)], bs)


def write_out(result, out, sem):
    copy = pltpu.make_async_copy(result, out, sem)
    copy.start()
    copy.wait()


def per_device(
    tokens, col_shift, frame_group, spatial_qkv, spatial_out, temporal_qkv, temporal_out
):
    smem = pl.BlockSpec(memory_space=pltpu.SMEM)
    anywhere = pl.BlockSpec(memory_space=pl.ANY)
    dma = pltpu.SemaphoreType.DMA
    result = pl.pallas_call(
        kernel,
        out_shape=pltpu.VMEM((8, 8, 8, D), BF16),
        in_specs=[smem, smem] + [anywhere] * 5,
        out_specs=pl.BlockSpec(memory_space=pltpu.VMEM),
        scratch_shapes=[
            pltpu.VMEM((D, 3 * D), BF16),
            pltpu.VMEM((D, D), BF16),
            pltpu.VMEM((D, 3 * D), BF16),
            pltpu.VMEM((D, D), BF16),
            pltpu.VMEM((D, D), BF16),
            pltpu.VMEM((D, D), BF16),
            pltpu.VMEM((8, 4, 8, D), BF16),
            pltpu.VMEM((8, 4, 8, D), BF16),
            pltpu.VMEM((256, D), BF16),
            pltpu.VMEM((256, 2 * D), BF16),
            pltpu.VMEM((2, 64, 2 * D), BF16),
            pltpu.VMEM((2, D, 128), BF16),
            pltpu.VMEM((6, 128, 9 * 128), BF16),
            pltpu.VMEM((64, 8, D), BF16),
            pltpu.VMEM((2, 4, 8, 8, D), BF16),
            pltpu.VMEM((2, 256, D), BF16),
            pltpu.VMEM((2, 256, 2 * D), BF16),
            pltpu.VMEM((2, 6, 128, 512), BF16),
            pltpu.VMEM((256, D), BF16),
            pltpu.VMEM((64, 8, D), BF16),
            pltpu.VMEM((64, GROUP), jnp.int32),
            dma((4,)),
            dma((8,)),
            dma,
            dma((8,)),
            dma,
            dma((2,)),
            dma,
            dma,
        ],
        compiler_params=pltpu.CompilerParams(
            collective_id=0, has_side_effects=True, vmem_limit_bytes=56 * 1024 * 1024
        ),
    )(
        col_shift,
        frame_group,
        tokens.reshape(8, 8, 8, D),
        spatial_qkv,
        spatial_out,
        temporal_qkv,
        temporal_out,
    )
    written = pl.pallas_call(
        write_out,
        out_shape=jax.ShapeDtypeStruct((8, 8, 8, D), BF16),
        in_specs=[anywhere],
        out_specs=anywhere,
        scratch_shapes=[dma],
    )(pltpu.with_memory_space_constraint(result, pltpu.VMEM))
    return written.reshape(tokens.shape)


def solution(mesh):
    in_specs = (P("tm", "rows", None, None), P("tm"), P(), P(), P(), P(), P())
    out_specs = P("tm", "rows", None, None)
    return jax.shard_map(
        per_device, mesh=mesh, in_specs=in_specs, out_specs=out_specs, check_vma=False
    )
```

```python
import functools

import jax
import jax.numpy as jnp
from jax import lax
from jax.experimental import pallas as pl
from jax.experimental.pallas import tpu as pltpu
from jax.sharding import PartitionSpec as P

D = 768
GROUP = 256
BF16 = jnp.bfloat16
F32 = jnp.float32
MESH = pl.DeviceIdType.MESH
AHEAD = 2
BEHIND = 2
FAR_FIRST = [(dy, dx, dc) for dy in (2, 1, 3, 0) for dx in (2, 1, 3, 0) for dc in (0, 1)]
FAR_FIRST.remove((0, 0, 0))
FAR_FIRST.sort(key=lambda d: -min(d[0], 4 - d[0]) - min(d[1], 4 - d[1]))


def iota(shape, dim):
    return lax.broadcasted_iota(jnp.int32, shape, dim)


def one_hot(mask):
    return jnp.where(mask, 1.0, 0.0).astype(BF16)


def layer_norm(x):
    center = x - jnp.mean(x, axis=-1, keepdims=True)
    spread = jnp.mean(center * center, axis=-1, keepdims=True)
    return (center * lax.rsqrt(spread + 1e-05)).astype(BF16)


def dot(a, b):
    return jnp.dot(a, b, preferred_element_type=F32)


def dot_t(a, b):
    return lax.dot_general(a, b, (((1,), (1,)), ((), ())), preferred_element_type=F32)


def block_diagonal(x):
    lane = iota(x.shape, 1) // 64
    return jnp.concatenate([jnp.where(lane == h, x, jnp.zeros_like(x)) for h in range(4)], axis=0)


def attend(s):
    e = jnp.exp((s - jnp.max(s, axis=0, keepdims=True)) * 0.125)
    return (e * (1.0 / jnp.sum(e, axis=0, keepdims=True))).astype(BF16)


def attend_all(bodies, allowed, same_head, extra=()):
    extra = list(extra)
    share = -(-len(extra) // len(bodies))
    def scores(body):
        s = dot_t(body[1](), block_diagonal(body[0]()))
        return s if allowed is None else jnp.where(allowed, s, -1e30)

    waiting, ready = [scores(body) for body in bodies[:AHEAD]], []
    for n, body in enumerate(bodies):
        if n + AHEAD < len(bodies):
            waiting.append(scores(bodies[n + AHEAD]))
        ready.append(attend(waiting[n]))
        if n >= BEHIND:
            mix_values(ready[n - BEHIND], *bodies[n - BEHIND][2:], same_head)
        for work in extra[n * share : n * share + share]:
            work()
    for n in range(len(bodies) - BEHIND, len(bodies)):
        mix_values(ready[n], *bodies[n][2:], same_head)


def mix_values(weights, values, slot, store, same_head):
    values = values()
    blank = jnp.zeros_like(weights)
    padded = jnp.concatenate([blank, weights] if slot else [weights, blank], axis=0)
    for p in range(2):
        lanes = slice(p * 128, p * 128 + 128)
        mixed = dot(values[lanes, :], padded[:, lanes])
        store(p, jnp.where(same_head, mixed, 0.0).astype(BF16))


def kernel(
    shift_ref, group_ref, tok, wsq_h, wso_h, wtq_h, wto_h, out,
    wsq, wso, wtq, wto, wsv, wtv, town, trcv, xin, qown, qrcv, values, mix, sbuf, rbuf, normed_t, qt,
    mixt, xout, obuf, mask, lsem, osem, zs, zr, fs, fr, bs, br,
):
    tm = lax.axis_index("tm")
    z = lax.axis_index("rows")
    core = lax.rem(tm, 2)
    x = lax.rem(tm // 2, 4)
    y = tm // 8
    zup = lax.rem(z + 1 + 6 * core, 8)
    zdown = lax.rem(z + 7 + 2 * core, 8)

    barrier = pltpu.get_barrier_semaphore()
    pl.semaphore_signal(barrier, inc=1, device_id=(tm, zup), device_id_type=MESH)

    loads = [
        pltpu.make_async_copy(src, dst, lsem.at[n])
        for n, (src, dst) in enumerate(((wsq_h, wsq), (wso_h, wso), (wtq_h, wtq), (wto_h, wto)))
    ]

    def own_copy(i):
        return pltpu.make_async_copy(
            tok.at[pl.ds(4 - 4 * core, 4), i], town.at[i], osem.at[i]
        )

    @pl.loop(0, 8)
    def _(i):
        own_copy(i).start()

    loads[0].start()

    @pl.loop(1, 32)
    def _(n):
        pl.semaphore_signal(
            barrier, inc=1, device_id=(lax.rem(tm + n, 32), z), device_id_type=MESH
        )

    sender_core = y // 2
    sender_z = lax.rem(z + 7 + 2 * sender_core, 8)

    @pl.loop(0, 16)
    def _(n):
        pl.semaphore_signal(
            barrier, inc=1, device_id=(2 * n + sender_core, sender_z), device_id_type=MESH
        )

    shift = shift_ref[0]

    rows, cols = iota((64, 96), 0), iota((64, 96), 1)
    gather = one_hot(
        (lax.rem(rows // 8, 4) == lax.rem(cols // 8, 4))
        & (8 * (cols // 32) + lax.rem(cols, 8) == 8 * (rows // 32) + lax.rem(rows, 8) + shift)
    )
    rows, cols = iota((128, 384), 0), iota((128, 384), 1)
    scatter = one_hot(
        (lax.rem(rows // 8, 8) == lax.rem(cols // 8, 8))
        & (8 * (rows // 64) + lax.rem(rows, 8) + 8 == 8 * (cols // 128) + lax.rem(cols, 8) + shift)
    )
    same_head = iota((128, 128), 0) // 64 == iota((128, 128), 1) // 64
    unit = one_hot(iota((GROUP, GROUP), 0) == iota((GROUP, GROUP), 1))

    def transpose_values(weight, result, i):
        rows_out = slice(i * GROUP, i * GROUP + GROUP)
        lanes = slice(2 * D + i * GROUP, 2 * D + i * GROUP + GROUP)
        for j in range(3):
            part = slice(j * GROUP, j * GROUP + GROUP)
            result[rows_out, part] = dot_t(unit, weight[part, lanes]).astype(BF16)

    def normed_pair(buffer, t):
        parts = []
        for b in range(3):
            parts.append(buffer[(2 * t + b) % 8 if isinstance(t, int) else lax.rem(2 * t + b, 8)].astype(F32).reshape(32, D))
        normed = layer_norm(jnp.concatenate(parts, axis=0))
        return dot(gather, normed).astype(BF16)

    @pl.loop(0, 8)
    def _(i):
        own_copy(i).wait()

    @pl.loop(0, 4)
    def _(t):
        xin[pl.ds(pl.multiple_of(t * 64, 64), 64), :] = normed_pair(town, t)

    pl.semaphore_wait(barrier, 48)

    def z_copy(i):
        return pltpu.make_async_remote_copy(
            src_ref=tok.at[pl.ds(4 * core, 4), i],
            dst_ref=trcv.at[i],
            send_sem=zs,
            recv_sem=zr.at[i],
            device_id=(tm, zdown),
            device_id_type=MESH,
        )

    @pl.loop(0, 8)
    def _(i):
        z_copy(i).start()

    loads[0].wait()
    for load in loads[1:]:
        load.start()

    def project_own(n):
        lanes = pl.ds(pl.multiple_of(n * GROUP, GROUP), GROUP)
        qown[:, lanes] = dot(xin[...], wsq[:, lanes]).astype(BF16)

    pl.loop(0, 6)(project_own)
    for i in range(3):
        transpose_values(wsq, wsv, i)

    for p in range(6):
        mix[p, :, 0:128] = jnp.zeros((128, 128), BF16)

    def build_mask():
        k_row, q_col = iota((64, 1), 0), lax.rem(iota((1, GROUP), 1), 64)

        def frame_of(n):
            m = lax.rem(n, 8)
            return (m // 2) * 8 + (n // 16) * 2 + lax.rem(m, 2)

        k_frame, q_frame = frame_of(k_row), frame_of(q_col)
        q_group, k_group = jnp.zeros_like(q_frame), jnp.zeros_like(k_frame)
        for f in range(32):
            value = group_ref[f]
            q_group = jnp.where(q_frame == f, value, q_group)
            k_group = jnp.where(k_frame == f, value, k_group)
        same = lax.rem(k_row // 8, 2) == lax.rem(q_col // 8, 2)
        mask[...] = jnp.where(same & (k_group <= q_group), 1, 0)

    loads[1].wait()

    own_row = 2 * y + x // 2

    def send_block(i):
        number = (i + 7) % 8
        r, side, low = number // 4, number // 2 % 2, number % 2
        place = rbuf.at[r, x, 2 * y + core]

        def send(h, row):
            half = core if h else 1 - core
            p = 4 * half + row
            target = ((p // 2) * 4 + 2 * lax.rem(p, 2) + low) * 2 + side
            return pltpu.make_async_remote_copy(
                src_ref=sbuf.at[i * 8 + h * 4 + row],
                dst_ref=place,
                send_sem=fs,
                recv_sem=fr.at[r],
                device_id=(target, zup if h else z),
                device_id_type=MESH,
            )

        for row in range(4):
            send(1, row).start()
        mine = lax.rem(own_row, 4)
        for n in range(1, 4):
            send(0, lax.rem(mine + n, 4)).start()
        here = (y // 2 == 1 - core) & (core == side) & (lax.rem(x, 2) == low)

        @pl.when(here)
        def _():
            pltpu.make_async_copy(sbuf.at[i * 8 + mine], place, fr.at[r]).start()

        @pl.when(jnp.logical_not(here))
        def _():
            send(0, mine).start()

    def finish_blocks(first, count, mixed, matrix):
        flat = jnp.concatenate([dot_t(matrix, part).astype(BF16) for part in mixed], axis=1)
        y_out = dot(flat, wso[...])
        residual = []
        for n in range(count):
            for buffer in (town, trcv):
                residual.append(buffer[first + n].astype(F32).reshape(32, D))
        stream = (jnp.concatenate(residual, axis=0) + y_out).astype(BF16)
        for n in range(count):
            for h in range(2):
                at = (2 * n + h) * 32
                for r in range(4):
                    sbuf[(first + n) * 8 + h * 4 + r] = stream[at + 8 * r : at + 8 * r + 8, :]

    def front(t):
        slot, pair = t % 2, []

        def norm():
            received = normed_pair(trcv, t)
            own_pair = xin[t * 64 : t * 64 + 64, :]
            pair.append(received)
            pair.append(
                jnp.concatenate(
                    [own_pair[:32], received[:32], own_pair[32:], received[32:]], axis=0
                )
            )

        def project(n):
            lanes = slice(n * GROUP, n * GROUP + GROUP)
            qrcv[slot, :, lanes] = dot(pair[0], wsq[:, lanes]).astype(BF16)

        def project_values(n):
            part_rows = slice(n * GROUP, n * GROUP + GROUP)
            values[slot, part_rows, :] = dot_t(wsv[part_rows, :], pair[1]).astype(BF16)

        work = [norm] + [functools.partial(project, n) for n in (0, 3, 1, 4, 2, 5)]
        return work + [functools.partial(project_values, n) for n in range(3)]

    def window(t, w, g):
        own_rows = slice(t * 64 + w * 32, t * 64 + w * 32 + 32)

        def part(n):
            lanes = slice(n * D + g * GROUP, n * D + g * GROUP + GROUP)
            received = qrcv[t % 2, w * 32 : w * 32 + 32, lanes]
            return jnp.concatenate([qown[own_rows, lanes], received], axis=0)

        def store(p, mixed):
            at = (2 * t + w + 1) * 128
            mix[2 * g + p, :, at : at + 128] = mixed

        def group_values():
            return values[t % 2, g * GROUP : g * GROUP + GROUP, :]

        return lambda: part(0), lambda: part(1), group_values, w, store

    for i in range(3):
        z_copy(i).wait_recv()
    for work in front(0):
        work()
    for t in range(4):
        for i in range(2 * t + 3, min(2 * t + 5, 8)):
            z_copy(i).wait_recv()
        bodies = [window(t, w, g) for w in range(2) for g in range(3)]
        if t < 3:
            extra = front(t + 1)
        else:
            loads[2].wait()
            extra = [functools.partial(transpose_values, wtq, wtv, i) for i in range(3)]
            extra.append(build_mask)
        attend_all(bodies, None, same_head, extra)
        recent = [mix[p, :, t * 256 : t * 256 + 384] for p in range(6)]
        finish_blocks(2 * t, 2, recent, scatter)
        if t:
            send_block(2 * t)
        send_block(2 * t + 1)

    edge = [jnp.concatenate([mix[p, :, 1024:1152], mix[p, :, 128:256]], axis=1) for p in range(6)]
    finish_blocks(0, 1, edge, scatter[:64, :256])
    send_block(0)

    loads[3].wait()
    rows, cols = iota((256, 256), 0), iota((256, 256), 1)
    regroup = one_hot(
        (rows // 64 == cols // 64)
        & (lax.rem(rows // 8, 8) == lax.rem(cols, 8))
        & (lax.rem(rows, 8) == lax.rem(cols // 8, 8))
    )
    rows, cols = iota((256, 512), 0), iota((256, 512), 1)
    swap = one_hot(
        (rows // 64 == lax.rem(cols // 16, 4))
        & (lax.rem(rows // 8, 8) == lax.rem(cols, 8))
        & (lax.rem(rows, 8) == 2 * (cols // 128) + lax.rem(cols // 8, 2))
    )

    def wait_bytes(ref, sem):
        pltpu.make_async_copy(ref, ref, sem).wait()

    def project_half(r):
        wait_bytes(rbuf.at[r], fr.at[r])
        normed = layer_norm(rbuf[r].astype(F32).reshape(256, D))
        normed_t[r] = dot(regroup, normed).astype(BF16)
        for m in range(6):
            lanes = slice(m * GROUP, m * GROUP + GROUP)
            qt[r, :, lanes] = dot(normed_t[r], wtq[:, lanes]).astype(BF16)

    def at(q, lp, s):
        first = s * 64 + q % 2 * 32 + lp * 16
        return slice(first, first + 16)

    def later(q):
        def project_values(n):
            tokens_pair = jnp.concatenate(
                [normed_t[q // 2, at(q, lp, s), :] for lp in range(2) for s in range(4)], axis=0
            )
            part_rows = slice(n * GROUP, n * GROUP + GROUP)
            values[q % 2, part_rows, :] = dot_t(wtv[part_rows, :], tokens_pair).astype(BF16)

        return [functools.partial(project_values, n) for n in range(3)]

    def location(q, lp, g):
        def part(n):
            lanes = slice(n * D + g * GROUP, n * D + g * GROUP + GROUP)
            return jnp.concatenate([qt[q // 2, at(q, lp, s), lanes] for s in range(4)], axis=0)

        def store(p, mixed):
            place = (2 * (q % 2) + lp) * 128
            mixt[q // 2, 2 * g + p, :, place : place + 128] = mixed

        def group_values():
            return values[q % 2, g * GROUP : g * GROUP + GROUP, :]

        return lambda: part(0), lambda: part(1), group_values, lp, store

    def give_back(r):
        for p in range(6):
            xout[:, p * 128 : p * 128 + 128] = dot_t(swap, mixt[r, p]).astype(BF16)
        for n in range(3):
            lanes = slice(n * GROUP, n * GROUP + GROUP)
            branch = dot(xout[...], wto[:, lanes])
            residual = rbuf[r, :, :, :, lanes].astype(F32).reshape(256, GROUP)
            result = (residual + branch).astype(BF16)
            for k in range(32):
                frame = (k % 8) // 2 * 8 + k // 8 * 2 + k % 2
                obuf[r * 32 + frame, :, lanes] = result[k * 8 : k * 8 + 8, :]

        place = out.at[own_row, lax.rem(r * 4 + core * 2 + lax.rem(x, 2) + 1, 8)]

        for dy, dx, dc in FAR_FIRST:
            target = (lax.rem(y + dy, 4) * 4 + lax.rem(x + dx, 4)) * 2 + lax.rem(core + dc, 2)
            pltpu.make_async_remote_copy(
                src_ref=obuf.at[r * 32 + target],
                dst_ref=place,
                send_sem=bs,
                recv_sem=br,
                device_id=(target, z),
                device_id_type=MESH,
            ).start()

        pltpu.make_async_copy(obuf.at[r * 32 + tm], place, br).start()

    for q in range(4):
        if q % 2 == 0:
            project_half(q // 2)
            for work in later(q):
                work()
        bodies = [location(q, lp, g) for lp in range(2) for g in range(3)]
        attend_all(bodies, mask[...] != 0, same_head, () if q % 2 else later(q + 1))
        if q % 2:
            give_back(q // 2)

    wait_bytes(out, br)
    wait_bytes(trcv, zs)
    local = y // 2 == 1 - core

    @pl.when(local)
    def _():
        wait_bytes(sbuf.at[pl.ds(0, 62)], fs)

    @pl.when(jnp.logical_not(local))
    def _():
        wait_bytes(sbuf, fs)

    wait_bytes(obuf.at[pl.ds(0, 62)], bs)


def write_out(result, out, sem):
    copies = [pltpu.make_async_copy(result.at[i], out.at[i], sem.at[i]) for i in range(8)]
    for copy in copies:
        copy.start()
    for copy in copies:
        copy.wait()


def per_device(
    tokens, col_shift, frame_group, spatial_qkv, spatial_out, temporal_qkv, temporal_out
):
    smem = pl.BlockSpec(memory_space=pltpu.SMEM)
    anywhere = pl.BlockSpec(memory_space=pl.ANY)
    dma = pltpu.SemaphoreType.DMA
    result = pl.pallas_call(
        kernel,
        out_shape=pltpu.VMEM((8, 8, 8, D), BF16),
        in_specs=[smem, smem] + [anywhere] * 5,
        out_specs=pl.BlockSpec(memory_space=pltpu.VMEM),
        scratch_shapes=[
            pltpu.VMEM((D, 3 * D), BF16),
            pltpu.VMEM((D, D), BF16),
            pltpu.VMEM((D, 3 * D), BF16),
            pltpu.VMEM((D, D), BF16),
            pltpu.VMEM((D, D), BF16),
            pltpu.VMEM((D, D), BF16),
            pltpu.VMEM((8, 4, 8, D), BF16),
            pltpu.VMEM((8, 4, 8, D), BF16),
            pltpu.VMEM((256, D), BF16),
            pltpu.VMEM((256, 2 * D), BF16),
            pltpu.VMEM((2, 64, 2 * D), BF16),
            pltpu.VMEM((2, D, 128), BF16),
            pltpu.VMEM((6, 128, 9 * 128), BF16),
            pltpu.VMEM((64, 8, D), BF16),
            pltpu.VMEM((2, 4, 8, 8, D), BF16),
            pltpu.VMEM((2, 256, D), BF16),
            pltpu.VMEM((2, 256, 2 * D), BF16),
            pltpu.VMEM((2, 6, 128, 512), BF16),
            pltpu.VMEM((256, D), BF16),
            pltpu.VMEM((64, 8, D), BF16),
            pltpu.VMEM((64, GROUP), jnp.int32),
            dma((4,)),
            dma((8,)),
            dma,
            dma((8,)),
            dma,
            dma((2,)),
            dma,
            dma,
        ],
        compiler_params=pltpu.CompilerParams(
            collective_id=0, has_side_effects=True, vmem_limit_bytes=56 * 1024 * 1024
        ),
    )(
        col_shift,
        frame_group,
        tokens.reshape(8, 8, 8, D),
        spatial_qkv,
        spatial_out,
        temporal_qkv,
        temporal_out,
    )
    written = pl.pallas_call(
        write_out,
        out_shape=jax.ShapeDtypeStruct((8, 8, 8, D), BF16),
        in_specs=[anywhere],
        out_specs=anywhere,
        scratch_shapes=[dma((8,))],
    )(pltpu.with_memory_space_constraint(result, pltpu.VMEM))
    return written.reshape(tokens.shape)


def solution(mesh):
    in_specs = (P("tm", "rows", None, None), P("tm"), P(), P(), P(), P(), P())
    out_specs = P("tm", "rows", None, None)
    return jax.shard_map(
        per_device, mesh=mesh, in_specs=in_specs, out_specs=out_specs, check_vma=False
    )
```
